256 devices in a mesh: space: 32 (over y, z), frag: 8 (over x, core).
Axes of the slice: x: 4, y: 4, z: 8, core: 2. Of those that a mesh axis runs over, the one named last changes fastest.
Arguments:
- latents: bfloat16 [1048576, 128], P(('space', 'frag')), may hold values from -6 to 6
- positions: float32 [3, 1048576], P(None, ('space', 'frag')), may hold values from 0 to 12
- masses: float32 [1048576], P(('space', 'frag')), may hold values from 0.5 to 2
- w_value: bfloat16 [128, 128], replicated, may hold values from -0.5 to 0.5
- w_self: bfloat16 [128, 128], replicated, may hold values from -0.5 to 0.5
- w_message: bfloat16 [128, 128], replicated, may hold values from -0.5 to 0.5
- w_offset: float32 [3, 128], replicated, may hold values from -3.5 to 3.5
- bias_hidden: float32 [128], replicated, may hold values from -3 to 3
- w_out: bfloat16 [128, 128], replicated, may hold values from -0.5 to 0.5
- norm_gain: float32 [128], replicated, may hold values from 0.1 to 1.9
- tile_blocks: int32 [2, 163840], P(None, ('space', 'frag')), may hold values from 0 to 39, as said below
- tile_count: int32 [256], P(('space', 'frag')), may hold values from 80 to 640, as said below
- send_rows: int32 [4, 65536], P(None, ('space', 'frag')), may hold values from 0 to 4095
- frag_ids: int32 [1048576], P(('space', 'frag')), may hold values from 0 to 1023
Outputs:
- updated: bfloat16 [1048576, 128], P(('space', 'frag'))
- pooled: float32 [1024, 128], P('frag')
The draws below stay inside these ranges and needn't reach their ends.
Inputs may be any that keep to these rules, and one draw needn't show every extreme that they name: `tile_blocks`: row 0 names a block of the device's own 32 blocks; row 1 names one of the 40 blocks of the extended rows. Only the first tile_count slots of a device are live; some device has all 640 live.
All inputs are finite; a program needn't handle non-finite values.
Results may differ from the reference program's by a relative error of at most 0.012.
Values may be sent and summed in bfloat16 or wider, within the bound.
A program may use at most 64 MiB of HBM per device.

```python
import math
import jax
import jax.numpy as jnp
from jax import lax

D = 128
HID = 128
TILE = 128
GROUP = 32
REACH = 2
HALO = 256
NODE_DEV = 4096
FR_DEV = 128
BLOCKS = 32
HALO_BLOCKS = 8
TILE_MAX = 640
PARTICLES = 1048576
FRAGMENTS = 1024
N_SPACE = 32
N_FRAG = 8
DEVICES = 256


def draw_positions(key, part):
    spread = jax.random.uniform(key, (3, PARTICLES), jnp.float32, 0.0, 1.0)
    return (12.0 * spread).astype(jnp.float32)


def draw_tile_blocks(key, part):
    keys = jax.random.split(key, 4)
    slots = DEVICES * TILE_MAX
    receiver = jax.random.randint(keys[0], (slots,), 0, BLOCKS)
    local_send = jax.random.randint(keys[1], (slots,), 0, BLOCKS)
    halo_send = BLOCKS + jax.random.randint(keys[2], (slots,), 0, HALO_BLOCKS)
    chooser = jax.random.randint(keys[3], (slots,), 0, 3)
    sender = jnp.where(chooser == 0, halo_send, local_send)
    return jnp.stack([receiver, sender]).astype(jnp.int32)


def draw_tile_count(key, part):
    keys = jax.random.split(key, 2)
    counts = jax.random.randint(keys[0], (DEVICES,), TILE_MAX // 8, TILE_MAX + 1)
    busiest = jax.random.randint(keys[1], (), 0, DEVICES)
    return jnp.where(jnp.arange(DEVICES) == busiest, TILE_MAX, counts).astype(jnp.int32)


def draw_frag_ids(key, part):
    keys = jax.random.split(key, 3)
    row_ids = jnp.arange(PARTICLES, dtype=jnp.int32)
    device = row_ids // NODE_DEV
    home = (device // N_FRAG + device % N_FRAG) % N_FRAG
    local_id = home * FR_DEV + jax.random.randint(keys[0], (PARTICLES,), 0, FR_DEV)
    spread_id = jax.random.randint(keys[1], (PARTICLES,), 0, FRAGMENTS)
    chooser = jax.random.randint(keys[2], (PARTICLES,), 0, 4)
    return jnp.where(chooser == 0, spread_id, local_id).astype(jnp.int32)


def set_ends(entries, own_key, least, high):
    dims = entries.shape
    index_at = [jax.random.randint(jax.random.fold_in(own_key, axis), (), 0, dims[axis]) for axis in range(len(dims))]
    entries = entries.at[tuple(index_at)].set(least)
    longest = dims.index(max(dims))
    index_at[longest] = (index_at[longest] + 1) % dims[longest]
    return entries.at[tuple(index_at)].set(high)


def shard_levels(rng, dims, shards, least, high):
    level = 1.0
    for axis_at, shards_of in shards:
        steps = jax.random.uniform(jax.random.fold_in(jax.random.fold_in(rng, 6), axis_at), (shards_of,), jnp.float32, least / len(shards), high / len(shards))
        level = level * jnp.repeat(jnp.exp(steps), dims[axis_at] // shards_of).reshape((-1,) + (1,) * (len(dims) - 1 - axis_at))
    return level


def gaussian(stream_key, extent, deviation, bound, cuts=(), kind=jnp.bfloat16):
    entries = deviation * jax.random.normal(stream_key, extent, jnp.float32)
    if cuts:
        entries = entries * shard_levels(stream_key, extent, cuts, -0.22, 0.18)
    return jnp.clip(entries, -bound, bound).astype(kind)


def setup_inputs(seed: int = 0) -> dict:
    splits = jax.random.split(jax.random.key(seed), 15)
    latents = gaussian(splits[0], (PARTICLES, D), 1.0, 6.0, ((0, 256),))
    positions = draw_positions(jax.random.fold_in(splits[14], 71), 0)
    masses = jnp.clip(jnp.exp(math.log(2.0) - 1.3862944 * jax.random.uniform(splits[2], (PARTICLES,), jnp.float32) ** shard_levels(splits[2], (PARTICLES,), ((0, 256),), -0.2, 0.2)), 0.5, 2.0)
    w_value = gaussian(splits[3], (D, D), D ** -0.5, 0.5)
    w_self = gaussian(splits[4], (D, HID), D ** -0.5, 0.5)
    w_message = gaussian(splits[5], (D, HID), D ** -0.5, 0.5)
    w_offset = gaussian(splits[6], (3, HID), 3 ** -0.5, 3.5, (), jnp.float32)
    bias_hidden = gaussian(splits[7], (HID,), 0.5, 3.0, (), jnp.float32)
    w_out = gaussian(splits[8], (HID, D), HID ** -0.5, 0.5)
    norm_gain = jnp.clip(1.0 + 0.18 * jax.random.normal(splits[9], (D,), jnp.float32), 0.1, 1.9)
    tile_blocks = draw_tile_blocks(jax.random.fold_in(splits[14], 71), 0)
    tile_count = draw_tile_count(jax.random.fold_in(splits[14], 71), 0)
    send_rows = set_ends(jax.random.randint(splits[12], (2 * REACH, DEVICES * HALO), 0, NODE_DEV), jax.random.fold_in(splits[12], 1), 0, NODE_DEV - 1).astype(jnp.int32)
    frag_ids = draw_frag_ids(jax.random.fold_in(splits[14], 71), 0)
    return {"latents": latents, "positions": positions, "masses": masses, "w_value": w_value, "w_self": w_self, "w_message": w_message, "w_offset": w_offset, "bias_hidden": bias_hidden, "w_out": w_out, "norm_gain": norm_gain, "tile_blocks": tile_blocks, "tile_count": tile_count, "send_rows": send_rows, "frag_ids": frag_ids}


norm_eps = 1e-05

def offsets_list():
    return [shift_by for shift_by in range(-REACH, REACH + 1) if shift_by != 0]

def tile_terms(running, group_id, blocks, live_tiles, ext_values, ext_pos, ext_mass, recv_blocks):
    message, moment, weight_sum = running
    first_slot = group_id * GROUP
    tile_index = first_slot + jnp.arange(GROUP, dtype=jnp.int32)
    receiver = lax.dynamic_slice_in_dim(blocks[0], first_slot, GROUP, 0)
    sender = lax.dynamic_slice_in_dim(blocks[1], first_slot, GROUP, 0)
    active = (tile_index < live_tiles).astype(jnp.float32)
    recv_pos = recv_blocks[receiver]
    send_pos = ext_pos[sender]
    squared = jnp.zeros((GROUP, TILE, TILE), jnp.float32)
    for c in range(3):
        delta = recv_pos[:, c, :, None] - send_pos[:, c, None, :]
        squared = squared + delta * delta
    distance = jnp.sqrt(squared)
    weight = (ext_mass[sender] * active[:, None])[:, None, :] * jnp.exp(-distance)
    rounded = lax.optimization_barrier(weight.astype(jnp.bfloat16)).astype(jnp.float32)
    sent_values = ext_values[sender].astype(jnp.float32)
    terms = jnp.einsum('gij,gjd->gid', rounded, sent_values)
    message = message.at[receiver].add(terms)
    moment = moment.at[receiver].add(jnp.einsum('gij,gcj->gci', weight, send_pos, precision=lax.Precision.HIGHEST))
    weight_sum = weight_sum.at[receiver].add(lax.optimization_barrier(jnp.sum(weight, axis=2)))
    return (message, moment, weight_sum)

def node_update(own_latents, own_pos, message, moment, weight_sum, w_self, w_message, w_offset, bias_hidden, w_out, norm_gain):
    rows = own_latents.shape[0]
    flat_sum = weight_sum.reshape(rows)
    aggregated = (message.reshape(rows, D) * lax.rsqrt(flat_sum)[:, None]).astype(jnp.bfloat16)
    centre = moment.transpose(1, 0, 2).reshape(3, rows) / flat_sum[None, :] - own_pos
    hidden_pre = jnp.dot(own_latents, w_self, preferred_element_type=jnp.float32)
    hidden_pre = hidden_pre + jnp.dot(aggregated, w_message, preferred_element_type=jnp.float32)
    for c in range(3):
        hidden_pre = hidden_pre + centre[c][:, None] * w_offset[c][None, :]
    hidden = jax.nn.silu(hidden_pre + bias_hidden[None, :]).astype(jnp.bfloat16)
    projected = jnp.dot(hidden, w_out, preferred_element_type=jnp.float32)
    row_mean = lax.optimization_barrier(jnp.mean(projected, axis=1, keepdims=True))
    centred = projected - row_mean
    row_var = lax.optimization_barrier(jnp.mean(centred * centred, axis=1, keepdims=True))
    normed = centred * lax.rsqrt(row_var + norm_eps) * norm_gain[None, :]
    return (own_latents.astype(jnp.float32) + normed).astype(jnp.bfloat16)

def reference(latents, positions, masses, w_value, w_self, w_message, w_offset, bias_hidden, w_out, norm_gain, tile_blocks, tile_count, send_rows, frag_ids):
    values = jnp.dot(latents, w_value, preferred_element_type=jnp.float32).astype(jnp.bfloat16)
    shifts_by = offsets_list()
    num_blocks = NODE_DEV // TILE

    def one_device(device):
        space_pos = device // N_FRAG
        frag_pos = device % N_FRAG
        first_row = device * NODE_DEV
        own_latents = lax.dynamic_slice_in_dim(latents, first_row, NODE_DEV, 0)
        own_values = lax.dynamic_slice_in_dim(values, first_row, NODE_DEV, 0)
        own_pos = lax.dynamic_slice_in_dim(positions, first_row, NODE_DEV, 1)
        own_mass = lax.dynamic_slice_in_dim(masses, first_row, NODE_DEV, 0)
        halo_values = [own_values]
        halo_pos = [own_pos]
        halo_mass = [own_mass]
        for k, shift_by in enumerate(shifts_by):
            source = space_pos - shift_by
            present = (source >= 0) & (source < N_SPACE)
            source_dev = (jnp.clip(source, 0, N_SPACE - 1) * N_FRAG + frag_pos).astype(jnp.int32)
            row_ids = lax.dynamic_slice_in_dim(send_rows[k], source_dev * HALO, HALO, 0) + source_dev * NODE_DEV
            halo_values.append(jnp.where(present, values[row_ids], jnp.zeros((), jnp.bfloat16)))
            halo_pos.append(jnp.where(present, positions[:, row_ids], jnp.zeros((), jnp.float32)))
            halo_mass.append(jnp.where(present, masses[row_ids], jnp.zeros((), jnp.float32)))
        ext_values = jnp.concatenate(halo_values, 0).reshape(-1, TILE, D)
        ext_pos = jnp.concatenate(halo_pos, 1).reshape(3, -1, TILE).transpose(1, 0, 2)
        ext_mass = jnp.concatenate(halo_mass, 0).reshape(-1, TILE)
        recv_blocks = own_pos.reshape(3, num_blocks, TILE).transpose(1, 0, 2)
        blocks = lax.dynamic_slice_in_dim(tile_blocks, device * TILE_MAX, TILE_MAX, 1)
        live_tiles = tile_count[device]
        initial = (jnp.zeros((num_blocks, TILE, D), jnp.float32), recv_blocks * own_mass.reshape(num_blocks, 1, TILE), own_mass.reshape(num_blocks, TILE))

        def advance(running, group_id):
            return (tile_terms(running, group_id, blocks, live_tiles, ext_values, ext_pos, ext_mass, recv_blocks), None)
        final, _ = lax.scan(advance, initial, jnp.arange(TILE_MAX // GROUP, dtype=jnp.int32))
        message, moment, weight_sum = final
        return node_update(own_latents, own_pos, message, moment, weight_sum, w_self, w_message, w_offset, bias_hidden, w_out, norm_gain)
    updated = lax.map(one_device, jnp.arange(DEVICES, dtype=jnp.int32)).reshape(PARTICLES, D)
    pool_scale = math.sqrt(FRAGMENTS / PARTICLES)
    pooled = jax.ops.segment_sum(updated.astype(jnp.float32), frag_ids, num_segments=FRAGMENTS) * pool_scale
    return (updated, pooled)
```

```python
import functools
import math

import jax
import jax.numpy as jnp
import numpy as np
from jax import lax
from jax.experimental import pallas as pl
from jax.experimental.pallas import tpu as pltpu
from jax.sharding import PartitionSpec as P

D = 128
TILE = 128
REACH = 2
HALO = 256
BLOCKS = 32
EXT = 40
NODE = BLOCKS * TILE
SLOTS = 640
FR_DEV = 128
OFFSETS = tuple(o for o in range(-REACH, REACH + 1) if o != 0)
LOG2E = math.log2(math.e)
CENTRE = 6.0
GROUP = 2
UNROLL = 8
NONE = -1e30

f32, bf16, i32 = jnp.float32, jnp.bfloat16, jnp.int32
MESH = pl.DeviceIdType.MESH


def split3(x):
    high = x.astype(bf16).astype(f32)
    rest = x - high
    mid = rest.astype(bf16).astype(f32)
    return high, mid, rest - mid


def feature_maps():
    recv = np.zeros((128, 32), np.float32)
    send = np.zeros((32, 16), np.float32)
    pairs = ((0, 0), (0, 1), (1, 0), (1, 1), (0, 2), (2, 0))
    for p, (a, b) in enumerate(pairs):
        for c in range(3):
            recv[3 * a + c, 3 * p + c] = -2.0
            send[3 * p + c, 3 * b + c] = 1.0
    for c in range(3):
        recv[13 + c, 18 + c] = 1.0
        send[18 + c, 12] = 1.0
        recv[12, 21 + c] = 1.0
        send[21 + c, 13 + c] = 1.0
    return jnp.asarray(recv, bf16), jnp.asarray(send, bf16)


def aux_columns(rows):
    cols = jnp.transpose(rows)
    return jnp.concatenate([cols, jnp.zeros((cols.shape[0], 112), f32)], axis=1).astype(bf16)


def halo_kernel(lat, pos, mass, wv, tb, tc, sr, fa, fb,
                A, B, V, lm, codes, lmult,
                rows_s, hot, sval, saux, rval, raux, ssem, rsem):
    s = lax.axis_index("space")
    f = lax.axis_index("frag")
    n_space = lax.axis_size("space")
    barrier = pltpu.get_barrier_semaphore()
    for o in OFFSETS:
        @pl.when((s + o >= 0) & (s + o < n_space))
        def _():
            pl.semaphore_signal(barrier, inc=1, device_id=(s + o, f), device_id_type=MESH)

    x = (pos[...] - CENTRE) * LOG2E
    xh, xm, xl = split3(x)
    mh, mm, ml = split3(mass[...])
    sq = x * x
    norm = sq[0:1] + sq[1:2] + sq[2:3]
    nh, nm, nl = split3(norm)
    rows = jnp.concatenate([xh, xm, xl, mh, mm, ml, jnp.ones((1, NODE), f32), nh, nm, nl], axis=0)
    rows_s[...] = rows
    for b in range(BLOCKS):
        V[b, :, 128:256] = aux_columns(rows_s[:, b * TILE:(b + 1) * TILE])
    values = jnp.dot(lat[...], wv[...], preferred_element_type=f32).astype(bf16)
    V[0:BLOCKS, :, 0:128] = values.reshape(BLOCKS, TILE, D)

    pl.semaphore_wait(barrier, jnp.minimum(s, REACH) + jnp.minimum(n_space - 1 - s, REACH))

    def copies(k):
        o = OFFSETS[k]
        dev = (s + o, f)
        return (
            pltpu.make_async_remote_copy(
                src_ref=sval.at[k], dst_ref=rval.at[k], send_sem=ssem.at[0, k], recv_sem=rsem.at[0, k],
                device_id=dev, device_id_type=MESH),
            pltpu.make_async_remote_copy(
                src_ref=saux.at[k], dst_ref=raux.at[k], send_sem=ssem.at[1, k], recv_sem=rsem.at[1, k],
                device_id=dev, device_id_type=MESH),
        )

    idx = sr[...].astype(f32)
    idx = jnp.transpose(jnp.concatenate([idx, idx], axis=0))
    lane = lax.broadcasted_iota(i32, (HALO, TILE), 1).astype(f32)
    table = V[0:BLOCKS].reshape(NODE, 256)
    for k in (0, 3, 1, 2):
        col = idx[:, k:k + 1]
        high = jnp.floor(col * (1.0 / TILE))
        low = col - high * TILE
        code = jnp.where(low == lane, high, -1.0).astype(bf16)
        for b in range(BLOCKS):
            hot[:, b * TILE:(b + 1) * TILE] = jnp.where(code == jnp.asarray(b, bf16), 1.0, 0.0).astype(bf16)
        got = jnp.dot(hot[...], table, preferred_element_type=f32)
        sval[k] = got[:, 0:128].astype(bf16)
        saux[k] = jnp.transpose(got[:, 128:256])[0:16].astype(bf16)
        o = OFFSETS[k]

        @pl.when((s + o >= 0) & (s + o < n_space))
        def _():
            for c in copies(k):
                c.start()

        @pl.when((s - o < 0) | (s - o >= n_space))
        def _():
            rval[k] = jnp.zeros((HALO, D), bf16)
            raux[k] = jnp.zeros((16, HALO), bf16)

    A[...] = jnp.dot(V[0:BLOCKS, :, 128:256].reshape(NODE, 128), fa[...],
                     preferred_element_type=f32).astype(bf16).reshape(BLOCKS, TILE, 32)
    rows = rows_s[...]
    own_b = jnp.dot(fb[...], rows.astype(bf16), preferred_element_type=f32).astype(bf16)
    lmass = jnp.log2(mass[...])
    for b in range(BLOCKS):
        B[b] = own_b[:, b * TILE:(b + 1) * TILE]
        lm[b] = lmass[:, b * TILE:(b + 1) * TILE]

    slot = lax.broadcasted_iota(i32, (BLOCKS, SLOTS), 1)
    rhot = (lax.broadcasted_iota(i32, (BLOCKS, SLOTS), 0) == tb[0:1, :]) & (slot < tc[0])
    chot = lax.broadcasted_iota(i32, (128, SLOTS), 0) == tb[1:2, :]
    count = lax.dot_general(
        jnp.where(rhot, 1.0, 0.0).astype(bf16), jnp.where(chot, 1.0, 0.0).astype(bf16),
        (((1,), (1,)), ((), ())), preferred_element_type=f32)
    live = jnp.where(count > 0.0, 1.0, 0.0)
    before = lax.broadcasted_iota(i32, (128, 128), 0) < lax.broadcasted_iota(i32, (128, 128), 1)
    place = jnp.dot(live.astype(bf16), jnp.where(before, 1.0, 0.0).astype(bf16), preferred_element_type=f32)
    place = jnp.where(count > 0.0, place, -1.0)
    col_id = lax.broadcasted_iota(i32, (BLOCKS, 128), 1).astype(f32)
    packed = col_id + 64.0 * count
    listed = jnp.zeros((BLOCKS, 128), f32)
    for c in range(EXT):
        listed = listed + jnp.where(place[:, c:c + 1] == col_id, packed[:, c:c + 1], 0.0)
    times = jnp.floor(listed * (1.0 / 64.0))
    sender = listed - 64.0 * times
    groups = jnp.maximum(jnp.floor((jnp.sum(live, axis=1, keepdims=True) + (GROUP - 1)) * (1.0 / GROUP)), 1.0)
    codes[...] = jnp.where(col_id == 127.0, groups, sender).astype(i32)
    lmult[...] = jnp.where(times > 0.0, jnp.log2(jnp.maximum(times, 1.0)), NONE)

    for k in (0, 3, 1, 2):
        o = OFFSETS[k]

        @pl.when((s - o >= 0) & (s - o < n_space))
        def _():
            for c in copies(k):
                c.wait_recv()

        aux = raux[k].astype(f32)
        V[BLOCKS + 2 * k:BLOCKS + 2 * k + 2, :, 0:128] = rval[k].reshape(2, TILE, D)
        V[BLOCKS + 2 * k:BLOCKS + 2 * k + 2, :, 128:256] = aux_columns(aux).reshape(2, TILE, 128)
        far_b = jnp.dot(fb[...], raux[k], preferred_element_type=f32).astype(bf16)
        far_mass = aux[9:10] + aux[10:11] + aux[11:12]
        far_lm = jnp.where(far_mass > 0.0, jnp.log2(jnp.maximum(far_mass, 1e-30)), NONE)
        for h in range(2):
            B[BLOCKS + 2 * k + h] = far_b[:, h * TILE:(h + 1) * TILE]
            lm[BLOCKS + 2 * k + h] = far_lm[:, h * TILE:(h + 1) * TILE]

    for k in range(4):
        o = OFFSETS[k]

        @pl.when((s + o >= 0) & (s + o < n_space))
        def _():
            for c in copies(k):
                c.wait_send()


def tile_kernel(codes, lmult, A, B, V, lm, lat, w_self, w_message, w_offset, bias, w_out, gain, ids,
                upd, part, acc, wb):
    acc[...] = jnp.zeros_like(acc)
    wb[...] = jnp.zeros_like(wb)
    total = lax.fori_loop(0, BLOCKS, lambda r, t: t + codes[r, 127], 0)

    def advance(state):
        out = []
        for _ in range(UNROLL):
            r, g = state
            over = g + 1 >= codes[r, 127]
            state = (jnp.minimum(jnp.where(over, r + 1, r), BLOCKS - 1), jnp.where(over, 0, g + 1))
            out.append(state)
        return out

    def step(it, states):
        now, last = states[:UNROLL], states[UNROLL:]
        for q in range(UNROLL):
            r, g = last[q]
            sent = jnp.concatenate([V[codes[r, g * GROUP + u]] for u in range(GROUP)], axis=0)
            acc[r] = acc[r] + jnp.dot(wb[q], sent, preferred_element_type=f32)
            r, g = now[q]
            off = jnp.where(it * UNROLL + q < total, 0.0, NONE).astype(f32)
            senders = [codes[r, g * GROUP + u] for u in range(GROUP)]
            sq = jnp.dot(A[r], jnp.concatenate([B[c] for c in senders], axis=1), preferred_element_type=f32)
            for u in range(GROUP):
                level = lm[senders[u]] + (lmult[r, g * GROUP + u] + off)
                d2 = jnp.maximum(sq[:, u * TILE:(u + 1) * TILE], 1e-12)
                wb[q, :, u * TILE:(u + 1) * TILE] = jnp.exp2(level - d2 * lax.rsqrt(d2)).astype(bf16)
        return tuple(advance(now[-1])) + tuple(now)

    zero = jnp.int32(0)
    first = [(zero, zero)] + advance((zero, zero))[:UNROLL - 1]
    lax.fori_loop(0, (total + UNROLL - 1) // UNROLL + 1, step, tuple(first) + ((zero, zero),) * UNROLL)

    ROWS = 512
    row_id = lax.broadcasted_iota(i32, (128, 128), 0)
    mass_map = jnp.where((row_id >= 9) & (row_id < 12), 1.0, 0.0).astype(bf16)
    woff = w_offset[...] * (1.0 / LOG2E)
    wh = woff.astype(bf16).astype(f32)
    wm = woff - wh
    pad = jnp.zeros((119, 128), f32)
    off_h = jnp.concatenate([wh, wh, wh, pad], axis=0).astype(bf16)
    off_m = jnp.concatenate([wm, wm, wm, pad], axis=0).astype(bf16)
    off_hh = jnp.concatenate([off_h, off_h], axis=0)
    w_sm = jnp.concatenate([w_self[...], w_message[...]], axis=0)
    wo = w_out[...].astype(f32)
    wc = wo - jnp.mean(wo, axis=1, keepdims=True)
    wc_h = wc.astype(bf16)
    wc_m = (wc - wc_h.astype(f32)).astype(bf16)
    wc2 = jnp.concatenate([wc_h, wc_m], axis=0)
    bias_row = bias[...]
    gain_row = gain[...]

    def node(i, _):
        blk = ROWS // TILE
        got = acc[pl.ds(i * blk, blk)].reshape(ROWS, 256)
        own_b = V[pl.ds(i * blk, blk), :, 128:256].reshape(ROWS, 128)
        mine = lat[pl.ds(pl.multiple_of(i * ROWS, ROWS), ROWS), :]
        own = own_b.astype(f32)
        m = jnp.dot(own_b, mass_map, preferred_element_type=f32)
        tot = got[:, 128:256] + m * own
        rs = lax.rsqrt(tot[:, 12:13])
        agg = (got[:, 0:128] * rs).astype(bf16)
        q = tot * (rs * rs) - own
        qh = q.astype(bf16)
        qm = (q - qh.astype(f32)).astype(bf16)
        pre = jnp.dot(jnp.concatenate([mine, agg], axis=1), w_sm, preferred_element_type=f32)
        pre = pre + jnp.dot(jnp.concatenate([qh, qm], axis=1), off_hh, preferred_element_type=f32)
        pre = pre + jnp.dot(qh, off_m, preferred_element_type=f32)
        pre = pre + bias_row
        hid = (pre * (0.5 + 0.5 * jnp.tanh(0.5 * pre))).astype(bf16)
        cen = jnp.dot(jnp.concatenate([hid, hid], axis=1), wc2, preferred_element_type=f32)
        var = jnp.mean(cen * cen, axis=1, keepdims=True)
        out = mine.astype(f32) + cen * lax.rsqrt(var + 1e-5) * gain_row
        upd[pl.ds(pl.multiple_of(i * ROWS, ROWS), ROWS), :] = out.astype(bf16)
        return 0

    lax.fori_loop(0, NODE // ROWS, node, 0)

    row = ids[...].astype(f32)
    high = jnp.floor(row * (1.0 / FR_DEV))
    low = row - high * FR_DEV
    sub = lax.broadcasted_iota(i32, (FR_DEV, NODE), 0).astype(f32).astype(bf16)
    for t in range(8):
        want = jnp.where(high == float(t), low, -1.0).astype(bf16)
        hot = jnp.where(jnp.broadcast_to(want, (FR_DEV, NODE)) == sub, 1.0, 0.0).astype(bf16)
        part[t] = jnp.dot(hot, upd[...], preferred_element_type=f32).astype(bf16)


def pool_kernel(scale, part, out, got1, mine, got2, full, s1, r1, s2, r2, s3, r3):
    s = lax.axis_index("space")
    f = lax.axis_index("frag")
    ns = lax.axis_size("space")
    nf = lax.axis_size("frag")
    barrier = pltpu.get_barrier_semaphore()

    def greet_f(i, _):
        pl.semaphore_signal(barrier, inc=1, device_id=(s, lax.rem(f + i, nf)), device_id_type=MESH)
        return 0

    def greet_s(i, _):
        pl.semaphore_signal(barrier, inc=1, device_id=(lax.rem(s + i, ns), f), device_id_type=MESH)
        return 0

    lax.fori_loop(1, nf, greet_f, 0)
    lax.fori_loop(1, ns, greet_s, 0)
    pl.semaphore_wait(barrier, nf + ns - 2)

    def copy1(i):
        to = lax.rem(f + i, nf)
        return pltpu.make_async_remote_copy(
            src_ref=part.at[to], dst_ref=got1.at[i - 1], send_sem=s1.at[i - 1], recv_sem=r1.at[i - 1],
            device_id=(s, to), device_id_type=MESH)

    def copy2(i):
        to = lax.rem(s + i, ns)
        return pltpu.make_async_remote_copy(
            src_ref=mine.at[to], dst_ref=got2.at[i - 1], send_sem=s2.at[i - 1], recv_sem=r2.at[i - 1],
            device_id=(to, f), device_id_type=MESH)

    def copy3(i):
        to = lax.rem(s + i, ns)
        return pltpu.make_async_remote_copy(
            src_ref=full.at[s], dst_ref=full.at[s], send_sem=s3.at[i - 1], recv_sem=r3.at[i - 1],
            device_id=(to, f), device_id_type=MESH)

    def each(n, fn):
        def body(i, _):
            fn(i)
            return 0
        lax.fori_loop(1, n, body, 0)

    each(nf, lambda i: copy1(i).start())
    each(nf, lambda i: copy1(i).wait_recv())
    total = part[f].astype(f32)
    for i in range(nf - 1):
        total = total + got1[i].astype(f32)
    mine[...] = total.reshape(ns, FR_DEV // ns, D)
    each(ns, lambda i: copy2(i).start())
    each(ns, lambda i: copy2(i).wait_recv())
    full[s] = (mine[s] + jnp.sum(got2[...], axis=0)) * scale
    each(ns, lambda i: copy3(i).start())
    each(ns, lambda i: copy3(i).wait_recv())
    out[...] = full[...].reshape(FR_DEV, D)
    each(nf, lambda i: copy1(i).wait_send())
    each(ns, lambda i: copy2(i).wait_send())
    each(ns, lambda i: copy3(i).wait_send())


def shards(latents, positions, masses, w_value, w_self, w_message, w_offset, bias_hidden, w_out, norm_gain,
           tile_blocks, tile_count, send_rows, frag_ids):
    ns, nf = lax.axis_size("space"), lax.axis_size("frag")
    vm = pl.BlockSpec(memory_space=pltpu.VMEM)
    sm = pl.BlockSpec(memory_space=pltpu.SMEM)
    fa, fb = feature_maps()
    dma = pltpu.SemaphoreType.DMA
    A, B, V, lm, codes, lmult = pl.pallas_call(
        halo_kernel,
        out_shape=(
            jax.ShapeDtypeStruct((BLOCKS, TILE, 32), bf16),
            jax.ShapeDtypeStruct((EXT, 32, TILE), bf16),
            jax.ShapeDtypeStruct((EXT, TILE, 256), bf16),
            jax.ShapeDtypeStruct((EXT, 1, TILE), f32),
            jax.ShapeDtypeStruct((BLOCKS, 128), i32),
            jax.ShapeDtypeStruct((BLOCKS, 128), f32),
        ),
        in_specs=[vm] * 5 + [sm] + [vm] * 3,
        out_specs=(vm,) * 6,
        scratch_shapes=[
            pltpu.VMEM((16, NODE), f32),
            pltpu.VMEM((HALO, NODE), bf16),
            pltpu.VMEM((4, HALO, D), bf16),
            pltpu.VMEM((4, 16, HALO), bf16),
            pltpu.VMEM((4, HALO, D), bf16),
            pltpu.VMEM((4, 16, HALO), bf16),
            dma((2, 4)),
            dma((2, 4)),
        ],
        compiler_params=pltpu.CompilerParams(
            collective_id=0, has_side_effects=True, vmem_limit_bytes=40 << 20),
    )(latents, positions, masses.reshape(1, NODE), w_value, tile_blocks, tile_count, send_rows, fa, fb)

    updated, part = pl.pallas_call(
        tile_kernel,
        out_shape=(
            jax.ShapeDtypeStruct((NODE, D), bf16),
            jax.ShapeDtypeStruct((nf, FR_DEV, D), bf16),
        ),
        in_specs=[sm, sm] + [vm] * 12,
        out_specs=(vm, vm),
        scratch_shapes=[
            pltpu.VMEM((BLOCKS, TILE, 256), f32),
            pltpu.VMEM((UNROLL, TILE, GROUP * TILE), bf16),
        ],
        compiler_params=pltpu.CompilerParams(vmem_limit_bytes=40 << 20),
    )(codes, lmult, A, B, V, lm, latents, w_self, w_message, w_offset, bias_hidden.reshape(1, D), w_out,
      norm_gain.reshape(1, D), frag_ids.reshape(1, NODE))

    scale = math.sqrt(FR_DEV * nf / (NODE * ns * nf))
    pooled = pl.pallas_call(
        functools.partial(pool_kernel, scale),
        out_shape=jax.ShapeDtypeStruct((FR_DEV, D), f32),
        in_specs=[vm],
        out_specs=vm,
        scratch_shapes=[
            pltpu.VMEM((nf - 1, FR_DEV, D), bf16),
            pltpu.VMEM((ns, FR_DEV // ns, D), f32),
            pltpu.VMEM((ns - 1, FR_DEV // ns, D), f32),
            pltpu.VMEM((ns, FR_DEV // ns, D), f32),
            dma((nf - 1,)), dma((nf - 1,)),
            dma((ns - 1,)), dma((ns - 1,)),
            dma((ns - 1,)), dma((ns - 1,)),
        ],
        compiler_params=pltpu.CompilerParams(collective_id=1, has_side_effects=True),
    )(part)
    return updated, pooled


def solution(mesh):
    own = P(("space", "frag"))
    return jax.shard_map(
        shards,
        mesh=mesh,
        in_specs=(
            P(("space", "frag"), None), P(None, ("space", "frag")), own,
            P(), P(), P(), P(), P(), P(), P(),
            P(None, ("space", "frag")), own, P(None, ("space", "frag")), own,
        ),
        out_specs=(P(("space", "frag"), None), P("frag", None)),
        check_vma=False,
    )
```

```python
import math

import jax
import jax.numpy as jnp
import numpy as np
from jax import lax
from jax.experimental import pallas as pl
from jax.experimental.pallas import tpu as pltpu
from jax.sharding import PartitionSpec as P

D = 128
TILE = 128
REACH = 2
HALO = 256
BLOCKS = 32
EXT = 40
NODE = BLOCKS * TILE
SLOTS = 640
FR_DEV = 128
OFFSETS = tuple(o for o in range(-REACH, REACH + 1) if o != 0)
LOG2E = math.log2(math.e)
CENTRE = 6.0
GROUP = 2
UNROLL = 8
NONE = -1e30

f32, bf16, i32 = jnp.float32, jnp.bfloat16, jnp.int32
MESH = pl.DeviceIdType.MESH


def split3(x):
    high = x.astype(bf16).astype(f32)
    rest = x - high
    mid = rest.astype(bf16).astype(f32)
    return high, mid, rest - mid


def feature_maps():
    recv = np.zeros((128, 32), np.float32)
    send = np.zeros((32, 16), np.float32)
    pairs = ((0, 0), (0, 1), (1, 0), (1, 1), (0, 2), (2, 0))
    for p, (a, b) in enumerate(pairs):
        for c in range(3):
            recv[3 * a + c, 3 * p + c] = -2.0
            send[3 * p + c, 3 * b + c] = 1.0
    for c in range(3):
        recv[13 + c, 18 + c] = 1.0
        send[18 + c, 12] = 1.0
        recv[12, 21 + c] = 1.0
        send[21 + c, 13 + c] = 1.0
    return jnp.asarray(recv, bf16), jnp.asarray(send, bf16)


def aux_columns(rows):
    cols = jnp.transpose(jnp.concatenate([rows, rows], axis=0))
    return jnp.concatenate([cols, jnp.zeros((cols.shape[0], 96), f32)], axis=1)


def halo_kernel(lat_h, pos_h, mass_h, wv_h, tb_h, tc, sr_h, fa_h, fb_h,
                ws_h, wmsg_h, woff_h, bias_h, wo_h, gain_h, ids_h,
                A, B, V, lm, codes, lmult, acc, lat, w_in, wc2, rows_out, want,
                pos, mass, wv, tb, sr, fa, fb, w_offset, w_out, ids,
                rows_s, hot, sval, saux, rval, raux, isem, ssem, rsem):
    s = lax.axis_index("space")
    f = lax.axis_index("frag")
    n_space = lax.axis_size("space")
    loads = [pltpu.make_async_copy(src, dst, isem.at[i]) for i, (src, dst) in enumerate((
        (pos_h, pos), (mass_h, mass), (lat_h, lat), (wv_h, wv), (sr_h, sr), (tb_h, tb), (fa_h, fa), (fb_h, fb),
        (ws_h, w_in.at[0:128]), (wmsg_h, w_in.at[128:256]), (woff_h, w_offset), (wo_h, w_out),
        (bias_h, rows_out.at[0:1]), (gain_h, rows_out.at[1:2]), (ids_h, ids)))]
    for c in loads:
        c.start()
    barrier = pltpu.get_barrier_semaphore()
    for o in OFFSETS:
        @pl.when((s + o >= 0) & (s + o < n_space))
        def _():
            pl.semaphore_signal(barrier, inc=1, device_id=(s + o, f), device_id_type=MESH)

    loads[0].wait()
    loads[1].wait()
    x = (pos[...] - CENTRE) * LOG2E
    xh, xm, xl = split3(x)
    mh, mm, ml = split3(mass[...])
    sq = x * x
    norm = sq[0:1] + sq[1:2] + sq[2:3]
    nh, nm, nl = split3(norm)
    rows_s[...] = jnp.concatenate([xh, xm, xl, mh, mm, ml, jnp.ones((1, NODE), f32), nh, nm, nl], axis=0)
    for b in range(BLOCKS):
        V[b, :, 128:256] = aux_columns(rows_s[:, b * TILE:(b + 1) * TILE]).astype(bf16)
    loads[2].wait()
    loads[3].wait()
    loads[4].wait()
    values = jnp.dot(lat[...], wv[...], preferred_element_type=f32).astype(bf16)
    V[0:BLOCKS, :, 0:128] = values.reshape(BLOCKS, TILE, D)

    def copies(k):
        o = OFFSETS[k]
        dev = (s + o, f)
        return (
            pltpu.make_async_remote_copy(
                src_ref=sval.at[k], dst_ref=rval.at[k], send_sem=ssem.at[0, k], recv_sem=rsem.at[0, k],
                device_id=dev, device_id_type=MESH),
            pltpu.make_async_remote_copy(
                src_ref=saux.at[k], dst_ref=raux.at[k], send_sem=ssem.at[1, k], recv_sem=rsem.at[1, k],
                device_id=dev, device_id_type=MESH),
        )

    idx = sr[...].astype(f32)
    idx = jnp.transpose(jnp.concatenate([idx, idx], axis=0))
    lane = lax.broadcasted_iota(i32, (HALO, TILE), 1).astype(f32)
    for first, pair in ((True, (0, 3)), (False, (1, 2))):
        for p, k in enumerate(pair):
            col = idx[:, k:k + 1]
            high = jnp.floor(col * (1.0 / TILE))
            low = col - high * TILE
            code = jnp.where(low == lane, high, -1.0).astype(bf16)
            for b in range(BLOCKS):
                hot[p * HALO:(p + 1) * HALO, b * TILE:(b + 1) * TILE] = jnp.where(
                    code == jnp.asarray(b, bf16), 1.0, 0.0).astype(bf16)
        got = jnp.dot(hot[...], V[0:BLOCKS].reshape(NODE, 256), preferred_element_type=f32)
        if first:
            pl.semaphore_wait(barrier, jnp.minimum(s, REACH) + jnp.minimum(n_space - 1 - s, REACH))
        for p, k in enumerate(pair):
            part = got[p * HALO:(p + 1) * HALO]
            sval[k] = part[:, 0:128].astype(bf16)
            saux[k] = jnp.transpose(part[:, 128:256])[0:16].astype(bf16)
            o = OFFSETS[k]

            @pl.when((s + o >= 0) & (s + o < n_space))
            def _():
                for c in copies(k):
                    c.start()

            @pl.when((s - o < 0) | (s - o >= n_space))
            def _():
                rval[k] = jnp.zeros((HALO, D), bf16)
                raux[k] = jnp.zeros((16, HALO), bf16)

    for c in loads[5:]:
        c.wait()
    slot = lax.broadcasted_iota(i32, (BLOCKS, SLOTS), 1)
    rhot = (lax.broadcasted_iota(i32, (BLOCKS, SLOTS), 0) == tb[0:1, :]) & (slot < tc[0])
    chot = lax.broadcasted_iota(i32, (128, SLOTS), 0) == tb[1:2, :]
    count = lax.dot_general(
        jnp.where(rhot, 1.0, 0.0).astype(bf16), jnp.where(chot, 1.0, 0.0).astype(bf16),
        (((1,), (1,)), ((), ())), preferred_element_type=f32)
    live = jnp.where(count > 0.0, 1.0, 0.0)
    before = lax.broadcasted_iota(i32, (128, 128), 0) < lax.broadcasted_iota(i32, (128, 128), 1)
    place = jnp.dot(live.astype(bf16), jnp.where(before, 1.0, 0.0).astype(bf16), preferred_element_type=f32)
    place = jnp.where(count > 0.0, place, -1.0)
    col_id = lax.broadcasted_iota(i32, (BLOCKS, 128), 1).astype(f32)
    packed = col_id + 64.0 * count
    listed = jnp.zeros((BLOCKS, 128), f32)
    for c in range(EXT):
        listed = listed + jnp.where(place[:, c:c + 1] == col_id, packed[:, c:c + 1], 0.0)
    times = jnp.floor(listed * (1.0 / 64.0))
    sender = listed - 64.0 * times
    groups = jnp.maximum(jnp.floor((jnp.sum(live, axis=1, keepdims=True) + (GROUP - 1)) * (1.0 / GROUP)), 1.0)
    codes[...] = jnp.where(col_id == 127.0, groups, sender).astype(i32)
    lmult[...] = jnp.where(times > 0.0, jnp.log2(jnp.maximum(times, 1.0)), NONE)

    A[...] = jnp.dot(V[0:BLOCKS, :, 128:256].reshape(NODE, 128), fa[...],
                     preferred_element_type=f32).astype(bf16).reshape(BLOCKS, TILE, 32)
    own_b = jnp.dot(fb[...], rows_s[...].astype(bf16), preferred_element_type=f32).astype(bf16)
    lmass = jnp.log2(mass[...])
    for b in range(BLOCKS):
        B[b] = own_b[:, b * TILE:(b + 1) * TILE]
        lm[b] = lmass[:, b * TILE:(b + 1) * TILE]

    fid = ids[...].astype(f32)
    high = jnp.floor(fid * (1.0 / FR_DEV))
    want[0:1] = high
    want[1:2] = fid - high * FR_DEV
    woff = w_offset[...] * (1.0 / LOG2E)
    wh = woff.astype(bf16).astype(f32)
    wm = woff - wh
    w_in[256:384] = jnp.concatenate(
        [wh, wh, wh, jnp.zeros((7, 128), f32), wm, wm, wm, jnp.zeros((103, 128), f32)], axis=0).astype(bf16)
    w_in[384:512] = jnp.concatenate([wh, wh, wh, jnp.zeros((119, 128), f32)], axis=0).astype(bf16)
    wo = w_out[...].astype(f32)
    wc = wo - jnp.mean(wo, axis=1, keepdims=True)
    wc_h = wc.astype(bf16)
    wc2[0:128] = wc_h
    wc2[128:256] = (wc - wc_h.astype(f32)).astype(bf16)

    row_id = lax.broadcasted_iota(i32, (128, 128), 0)
    mass_map = jnp.where((row_id >= 9) & (row_id < 12), 1.0, 0.0).astype(bf16)
    for b in range(BLOCKS):
        own = V[b, :, 128:256]
        acc[b, :, 0:128] = jnp.zeros((TILE, 128), f32)
        acc[b, :, 128:256] = jnp.dot(own, mass_map, preferred_element_type=f32) * own.astype(f32)

    for k in (0, 3, 1, 2):
        o = OFFSETS[k]

        @pl.when((s - o >= 0) & (s - o < n_space))
        def _():
            for c in copies(k):
                c.wait_recv()

        aux = raux[k].astype(f32)
        V[BLOCKS + 2 * k:BLOCKS + 2 * k + 2, :, 0:128] = rval[k].reshape(2, TILE, D)
        V[BLOCKS + 2 * k:BLOCKS + 2 * k + 2, :, 128:256] = aux_columns(aux).astype(bf16).reshape(2, TILE, 128)
        far_b = jnp.dot(fb[...], raux[k], preferred_element_type=f32).astype(bf16)
        far_mass = aux[9:10] + aux[10:11] + aux[11:12]
        far_lm = jnp.where(far_mass > 0.0, jnp.log2(jnp.maximum(far_mass, 1e-30)), NONE)
        for h in range(2):
            B[BLOCKS + 2 * k + h] = far_b[:, h * TILE:(h + 1) * TILE]
            lm[BLOCKS + 2 * k + h] = far_lm[:, h * TILE:(h + 1) * TILE]

    for k in range(4):
        o = OFFSETS[k]

        @pl.when((s + o >= 0) & (s + o < n_space))
        def _():
            for c in copies(k):
                c.wait_send()


def tile_kernel(codes, lmult, A, B, V, lm, acc_in, lat, w_in, wc2, rows, acc, upd_h, upd, wb, osem):
    wb[...] = jnp.zeros_like(wb)
    total = lax.fori_loop(0, BLOCKS, lambda r, t: t + codes[r, 127], 0)

    def advance(state):
        out = []
        for _ in range(UNROLL):
            r, g = state
            over = g + 1 >= codes[r, 127]
            state = (jnp.minimum(jnp.where(over, r + 1, r), BLOCKS - 1), jnp.where(over, 0, g + 1))
            out.append(state)
        return out

    def step(it, states):
        now, last = states[:UNROLL], states[UNROLL:]
        for q in range(UNROLL):
            r, g = last[q]
            sent = jnp.concatenate([V[codes[r, g * GROUP + u]] for u in range(GROUP)], axis=0)
            acc[r] = acc[r] + jnp.dot(wb[q], sent, preferred_element_type=f32)
            r, g = now[q]
            off = jnp.where(it * UNROLL + q < total, 0.0, NONE).astype(f32)
            senders = [codes[r, g * GROUP + u] for u in range(GROUP)]
            sq = jnp.dot(A[r], jnp.concatenate([B[c] for c in senders], axis=1), preferred_element_type=f32)
            for u in range(GROUP):
                level = lm[senders[u]] + (lmult[r, g * GROUP + u] + off)
                d2 = jnp.maximum(sq[:, u * TILE:(u + 1) * TILE], 1e-12)
                wb[q, :, u * TILE:(u + 1) * TILE] = jnp.exp2(level - d2 * lax.rsqrt(d2)).astype(bf16)
        return tuple(advance(now[-1])) + tuple(now)

    zero = jnp.int32(0)
    first = [(zero, zero)] + advance((zero, zero))[:UNROLL - 1]
    lax.fori_loop(0, (total + UNROLL - 1) // UNROLL + 1, step, tuple(first) + ((zero, zero),) * UNROLL)

    bias_row = rows[0:1]
    gain_row = rows[1:2]
    PIECES = 8
    outs = [pltpu.make_async_copy(upd.at[pl.ds(i * (NODE // PIECES), NODE // PIECES)],
                                  upd_h.at[pl.ds(i * (NODE // PIECES), NODE // PIECES)], osem.at[i])
            for i in range(PIECES)]

    def stage1(b):
        tot = acc[b, :, 128:256]
        rs = lax.rsqrt(tot[:, 12:13])
        agg = (acc[b, :, 0:128] * rs).astype(bf16)
        q = tot * (rs * rs) - V[b, :, 128:256].astype(f32)
        qh = q.astype(bf16)
        qm = (q - qh.astype(f32)).astype(bf16)
        return jnp.concatenate([lat[b * TILE:(b + 1) * TILE], agg, qh, qm], axis=1)

    def stage2(cat):
        pre = jnp.dot(cat, w_in[...], preferred_element_type=f32) + bias_row
        hid = (pre * (0.5 + 0.5 * jnp.tanh(0.5 * pre))).astype(bf16)
        return jnp.concatenate([hid, hid], axis=1)

    def stage3(b, hid):
        cen = jnp.dot(hid, wc2[...], preferred_element_type=f32)
        var = jnp.mean(cen * cen, axis=1, keepdims=True)
        out = lat[b * TILE:(b + 1) * TILE].astype(f32) + cen * lax.rsqrt(var + 1e-5) * gain_row
        upd[b * TILE:(b + 1) * TILE] = out.astype(bf16)

    cats, hids = {}, {}
    for b in range(BLOCKS + 2):
        if b >= 2:
            stage3(b - 2, hids.pop(b - 2))
            if (b - 1) % (BLOCKS // PIECES) == 0:
                outs[(b - 2) // (BLOCKS // PIECES)].start()
        if 1 <= b <= BLOCKS:
            hids[b - 1] = stage2(cats.pop(b - 1))
        if b < BLOCKS:
            cats[b] = stage1(b)
    for c in outs:
        c.wait()


NZ = 8
NY = 4


def pool_kernel(upd, want, out, hot, part, g1, a2, g2, a3, g3, full, s1, r1, s2, r2, s3, r3, s4, r4):
    s = lax.axis_index("space")
    f = lax.axis_index("frag")
    nf = lax.axis_size("frag")
    y = s // NZ
    z = lax.rem(s, NZ)
    barrier = pltpu.get_barrier_semaphore()

    def dev(dy, dz, df):
        return (lax.rem(y + dy, NY) * NZ + lax.rem(z + dz, NZ), lax.rem(f + df, nf))

    peers = [dev(0, 0, i) for i in range(1, nf)] + [dev(i, 0, 0) for i in range(1, NY)]
    peers += [dev(0, i, 0) for i in range(1, NZ)]
    for p in peers:
        pl.semaphore_signal(barrier, inc=1, device_id=p, device_id_type=MESH)

    def remote(src, dst, send, recv, i, to):
        return pltpu.make_async_remote_copy(
            src_ref=src, dst_ref=dst, send_sem=send.at[i - 1], recv_sem=recv.at[i - 1],
            device_id=to, device_id_type=MESH)

    c1 = {i: remote(part.at[i], g1.at[i - 1], s1, r1, i, dev(0, 0, i)) for i in range(1, nf)}
    c2 = {i: remote(a2.at[lax.rem(y + i, NY)], g2.at[i - 1], s2, r2, i, dev(i, 0, 0)) for i in range(1, NY)}
    c3 = {i: remote(a3, g3.at[i - 1], s3, r3, i, dev(0, i, 0)) for i in range(1, NZ)}
    c4 = {i: remote(full.at[y], full.at[y], s4, r4, i, dev(i, 0, 0)) for i in range(1, NY)}

    sub = lax.broadcasted_iota(i32, (FR_DEV, TILE), 0).astype(f32).astype(bf16)
    high = want[0:1]
    low = want[1:2]

    def build(slot, i):
        t = lax.rem(f + i, nf).astype(f32)
        row = jnp.where(high == t, low, -1.0).astype(bf16)
        for b in range(BLOCKS):
            cut = jnp.broadcast_to(row[:, b * TILE:(b + 1) * TILE], (FR_DEV, TILE))
            hot[slot, :, b * TILE:(b + 1) * TILE] = jnp.where(cut == sub, 1.0, 0.0).astype(bf16)

    order = (4, 3, 5, 2, 6, 1, 7, 0)
    build(0, order[0])
    for n, i in enumerate(order):
        if n + 1 < nf:
            build((n + 1) % 2, order[n + 1])
        sums = jnp.dot(hot[n % 2], upd[...], preferred_element_type=f32)
        if n == 0:
            pl.semaphore_wait(barrier, nf + NY + NZ - 3)
        if i:
            part[i] = sums.astype(bf16)
            c1[i].start()
        else:
            total = sums
    for i in order[:-1]:
        c1[i].wait_recv()
        total = total + g1[i - 1].astype(f32)
    a2[...] = total.astype(bf16).reshape(NY, FR_DEV // NY, D)
    for i in (2, 1, 3):
        c2[i].start()
    total = a2[y].astype(f32)
    for i in (1, 3, 2):
        c2[i].wait_recv()
        total = total + g2[i - 1].astype(f32)
    a3[...] = total.astype(bf16)
    for i in (4, 3, 5, 2, 6, 1, 7):
        c3[i].start()
    total = a3[...].astype(f32)
    for i in (1, 7, 2, 6, 3, 5, 4):
        c3[i].wait_recv()
        total = total + g3[i - 1].astype(f32)
    full[y] = total
    for i in (2, 1, 3):
        c4[i].start()
    for i in (1, 3, 2):
        c4[i].wait_recv()
    out[...] = full[...].reshape(FR_DEV, D)
    for group in (c1, c2, c3, c4):
        for c in group.values():
            c.wait_send()


def shards(latents, positions, masses, w_value, w_self, w_message, w_offset, bias_hidden, w_out, norm_gain,
           tile_blocks, tile_count, send_rows, frag_ids):
    ns, nf = lax.axis_size("space"), lax.axis_size("frag")
    vm = pl.BlockSpec(memory_space=pltpu.VMEM)
    sm = pl.BlockSpec(memory_space=pltpu.SMEM)
    hbm = pl.BlockSpec(memory_space=pltpu.HBM)
    fa, fb = feature_maps()
    dma = pltpu.SemaphoreType.DMA
    vmem = pltpu.VMEM
    limit = 36 << 20
    pin = lambda a: pltpu.with_memory_space_constraint(a, pltpu.HBM)
    A, B, V, lm, codes, lmult, acc, lat, w_in, wc2, rows, want = pl.pallas_call(
        halo_kernel,
        out_shape=(
            jax.ShapeDtypeStruct((BLOCKS, TILE, 32), bf16),
            jax.ShapeDtypeStruct((EXT, 32, TILE), bf16),
            jax.ShapeDtypeStruct((EXT, TILE, 256), bf16),
            jax.ShapeDtypeStruct((EXT, 1, TILE), f32),
            jax.ShapeDtypeStruct((BLOCKS, 128), i32),
            jax.ShapeDtypeStruct((BLOCKS, 128), f32),
            jax.ShapeDtypeStruct((BLOCKS, TILE, 256), f32),
            jax.ShapeDtypeStruct((NODE, D), bf16),
            jax.ShapeDtypeStruct((512, D), bf16),
            jax.ShapeDtypeStruct((256, D), bf16),
            jax.ShapeDtypeStruct((2, D), f32),
            jax.ShapeDtypeStruct((2, NODE), f32),
        ),
        in_specs=[hbm] * 5 + [sm] + [hbm] * 10,
        out_specs=(vm,) * 12,
        scratch_shapes=[
            vmem((3, NODE), f32), vmem((1, NODE), f32), vmem((D, D), bf16),
            vmem((2, SLOTS), i32), vmem((4, HALO), i32), vmem((128, 32), bf16), vmem((32, 16), bf16),
            vmem((3, D), f32), vmem((D, D), bf16), vmem((1, NODE), i32),
            vmem((16, NODE), f32),
            vmem((2 * HALO, NODE), bf16),
            vmem((4, HALO, D), bf16),
            vmem((4, 16, HALO), bf16),
            vmem((4, HALO, D), bf16),
            vmem((4, 16, HALO), bf16),
            dma((15,)),
            dma((2, 4)),
            dma((2, 4)),
        ],
        compiler_params=pltpu.CompilerParams(collective_id=0, has_side_effects=True, vmem_limit_bytes=limit),
    )(pin(latents), pin(positions), pin(masses.reshape(1, NODE)), pin(w_value), pin(tile_blocks), tile_count,
      pin(send_rows), pin(fa), pin(fb),
      pin(w_self), pin(w_message), pin(w_offset), pin(bias_hidden.reshape(1, D)), pin(w_out),
      pin(norm_gain.reshape(1, D)),
      pin(frag_ids.reshape(1, NODE)))

    _, updated, upd = pl.pallas_call(
        tile_kernel,
        out_shape=(
            jax.ShapeDtypeStruct((BLOCKS, TILE, 256), f32),
            jax.ShapeDtypeStruct((NODE, D), bf16),
            jax.ShapeDtypeStruct((NODE, D), bf16),
        ),
        in_specs=[sm, sm] + [vm] * 9,
        out_specs=(vm, hbm, vm),
        input_output_aliases={6: 0},
        scratch_shapes=[vmem((UNROLL, TILE, GROUP * TILE), bf16), dma((8,))],
        compiler_params=pltpu.CompilerParams(vmem_limit_bytes=limit),
    )(codes, lmult, A, B, V, lm, acc, lat, w_in, wc2, rows)

    pooled = pl.pallas_call(
        pool_kernel,
        out_shape=jax.ShapeDtypeStruct((FR_DEV, D), f32),
        in_specs=[vm, vm],
        out_specs=vm,
        scratch_shapes=[
            vmem((2, FR_DEV, NODE), bf16),
            vmem((nf, FR_DEV, D), bf16),
            vmem((nf - 1, FR_DEV, D), bf16),
            vmem((NY, FR_DEV // NY, D), bf16),
            vmem((NY - 1, FR_DEV // NY, D), bf16),
            vmem((FR_DEV // NY, D), bf16),
            vmem((NZ - 1, FR_DEV // NY, D), bf16),
            vmem((NY, FR_DEV // NY, D), f32),
            dma((nf - 1,)), dma((nf - 1,)),
            dma((NY - 1,)), dma((NY - 1,)),
            dma((NZ - 1,)), dma((NZ - 1,)),
            dma((NY - 1,)), dma((NY - 1,)),
        ],
        compiler_params=pltpu.CompilerParams(collective_id=1, has_side_effects=True, vmem_limit_bytes=limit),
    )(upd, want)
    return updated, pooled * math.sqrt(FR_DEV * nf / (NODE * ns * nf))


def solution(mesh):
    own = P(("space", "frag"))
    return jax.shard_map(
        shards,
        mesh=mesh,
        in_specs=(
            P(("space", "frag"), None), P(None, ("space", "frag")), own,
            P(), P(), P(), P(), P(), P(), P(),
            P(None, ("space", "frag")), own, P(None, ("space", "frag")), own,
        ),
        out_specs=(P(("space", "frag"), None), P("frag", None)),
        check_vma=False,
    )
```

```python
import math

import jax
import jax.numpy as jnp
import numpy as np
from jax import lax
from jax.experimental import pallas as pl
from jax.experimental.pallas import tpu as pltpu
from jax.sharding import PartitionSpec as P

D = 128
TILE = 128
REACH = 2
HALO = 256
BLOCKS = 32
EXT = 40
NODE = BLOCKS * TILE
SLOTS = 640
FR_DEV = 128
OFFSETS = tuple(o for o in range(-REACH, REACH + 1) if o != 0)
LOG2E = math.log2(math.e)
CENTRE = 6.0
GROUP = 2
UNROLL = 16
NONE = -1e30

f32, bf16, i32 = jnp.float32, jnp.bfloat16, jnp.int32
MESH = pl.DeviceIdType.MESH


def split3(x):
    high = x.astype(bf16).astype(f32)
    rest = x - high
    mid = rest.astype(bf16).astype(f32)
    return high, mid, rest - mid


def feature_maps():
    recv = np.zeros((128, 32), np.float32)
    send = np.zeros((32, 16), np.float32)
    pairs = ((0, 0), (0, 1), (1, 0), (1, 1), (0, 2), (2, 0))
    for p, (a, b) in enumerate(pairs):
        for c in range(3):
            recv[3 * a + c, 3 * p + c] = -2.0
            send[3 * p + c, 3 * b + c] = 1.0
    for c in range(3):
        recv[13 + c, 18 + c] = 1.0
        send[18 + c, 12] = 1.0
        recv[12, 21 + c] = 1.0
        send[21 + c, 13 + c] = 1.0
    return jnp.asarray(recv, bf16), jnp.asarray(send, bf16)


def aux_columns(rows):
    cols = jnp.transpose(jnp.concatenate([rows, rows], axis=0))
    return jnp.concatenate([cols, jnp.zeros((cols.shape[0], 96), f32)], axis=1)


def halo_kernel(lat_h, pos_h, mass_h, wv_h, tb_h, tc, sr_h, fa_h, fb_h,
                ws_h, wmsg_h, woff_h, bias_h, wo_h, gain_h, ids_h,
                A, B, V, lm, codes, lmult, acc, lat, w_in, wc2, rows_out, want,
                pos, mass, wv, tb, sr, fa, fb, w_offset, w_out, ids,
                rows_s, hot, sval, saux, rval, raux, isem, ssem, rsem):
    s = lax.axis_index("space")
    f = lax.axis_index("frag")
    n_space = lax.axis_size("space")
    loads = [pltpu.make_async_copy(src, dst, isem.at[i]) for i, (src, dst) in enumerate((
        (sr_h, sr), (pos_h, pos), (mass_h, mass), (lat_h, lat), (wv_h, wv), (tb_h, tb), (fa_h, fa), (fb_h, fb),
        (ws_h, w_in.at[0:128]), (wmsg_h, w_in.at[128:256]), (woff_h, w_offset), (wo_h, w_out),
        (bias_h, rows_out.at[0:1]), (gain_h, rows_out.at[1:2]), (ids_h, ids)))]
    for c in loads:
        c.start()
    barrier = pltpu.get_barrier_semaphore()
    for o in OFFSETS:
        @pl.when((s + o >= 0) & (s + o < n_space))
        def _():
            pl.semaphore_signal(barrier, inc=1, device_id=(s + o, f), device_id_type=MESH)

    loads[1].wait()
    loads[2].wait()
    x = (pos[...] - CENTRE) * LOG2E
    xh, xm, xl = split3(x)
    mh, mm, ml = split3(mass[...])
    sq = x * x
    norm = sq[0:1] + sq[1:2] + sq[2:3]
    nh, nm, nl = split3(norm)
    rows_s[...] = jnp.concatenate([xh, xm, xl, mh, mm, ml, jnp.ones((1, NODE), f32), nh, nm, nl], axis=0)
    for b in range(BLOCKS):
        V[b, :, 128:256] = aux_columns(rows_s[:, b * TILE:(b + 1) * TILE]).astype(bf16)
    loads[3].wait()
    loads[4].wait()
    loads[0].wait()
    values = jnp.dot(lat[...], wv[...], preferred_element_type=f32).astype(bf16)
    V[0:BLOCKS, :, 0:128] = values.reshape(BLOCKS, TILE, D)

    def copies(k):
        o = OFFSETS[k]
        dev = (s + o, f)
        return (
            pltpu.make_async_remote_copy(
                src_ref=sval.at[k], dst_ref=rval.at[k], send_sem=ssem.at[0, k], recv_sem=rsem.at[0, k],
                device_id=dev, device_id_type=MESH),
            pltpu.make_async_remote_copy(
                src_ref=saux.at[k], dst_ref=raux.at[k], send_sem=ssem.at[1, k], recv_sem=rsem.at[1, k],
                device_id=dev, device_id_type=MESH),
        )

    idx = sr[...].astype(f32)
    idx = jnp.transpose(jnp.concatenate([idx, idx], axis=0))
    lane = lax.broadcasted_iota(i32, (HALO, TILE), 1).astype(f32)
    for first, pair in ((True, (0, 3)), (False, (1, 2))):
        for p, k in enumerate(pair):
            col = idx[:, k:k + 1]
            high = jnp.floor(col * (1.0 / TILE))
            low = col - high * TILE
            code = jnp.where(low == lane, high, -1.0).astype(bf16)
            for b in range(BLOCKS):
                hot[p * HALO:(p + 1) * HALO, b * TILE:(b + 1) * TILE] = jnp.where(
                    code == jnp.asarray(b, bf16), 1.0, 0.0).astype(bf16)
        got = jnp.dot(hot[...], V[0:BLOCKS].reshape(NODE, 256), preferred_element_type=f32)
        if first:
            pl.semaphore_wait(barrier, jnp.minimum(s, REACH) + jnp.minimum(n_space - 1 - s, REACH))
        for p, k in enumerate(pair):
            part = got[p * HALO:(p + 1) * HALO]
            sval[k] = part[:, 0:128].astype(bf16)
            saux[k] = jnp.transpose(part[:, 128:256])[0:16].astype(bf16)
            o = OFFSETS[k]

            @pl.when((s + o >= 0) & (s + o < n_space))
            def _():
                for c in copies(k):
                    c.start()

            @pl.when((s - o < 0) | (s - o >= n_space))
            def _():
                rval[k] = jnp.zeros((HALO, D), bf16)
                raux[k] = jnp.zeros((16, HALO), bf16)

    for c in loads[5:]:
        c.wait()
    slot = lax.broadcasted_iota(i32, (BLOCKS, SLOTS), 1)
    rhot = (lax.broadcasted_iota(i32, (BLOCKS, SLOTS), 0) == tb[0:1, :]) & (slot < tc[0])
    chot = lax.broadcasted_iota(i32, (128, SLOTS), 0) == tb[1:2, :]
    count = lax.dot_general(
        jnp.where(rhot, 1.0, 0.0).astype(bf16), jnp.where(chot, 1.0, 0.0).astype(bf16),
        (((1,), (1,)), ((), ())), preferred_element_type=f32)
    live = jnp.where(count > 0.0, 1.0, 0.0)
    before = lax.broadcasted_iota(i32, (128, 128), 0) < lax.broadcasted_iota(i32, (128, 128), 1)
    place = jnp.dot(live.astype(bf16), jnp.where(before, 1.0, 0.0).astype(bf16), preferred_element_type=f32)
    place = jnp.where(count > 0.0, place, -1.0)
    col_id = lax.broadcasted_iota(i32, (BLOCKS, 128), 1).astype(f32)
    packed = col_id + 64.0 * count
    listed = jnp.zeros((BLOCKS, 128), f32)
    for c in range(EXT):
        listed = listed + jnp.where(place[:, c:c + 1] == col_id, packed[:, c:c + 1], 0.0)
    times = jnp.floor(listed * (1.0 / 64.0))
    sender = listed - 64.0 * times
    groups = jnp.maximum(jnp.floor((jnp.sum(live, axis=1, keepdims=True) + (GROUP - 1)) * (1.0 / GROUP)), 1.0)
    codes[...] = jnp.where(col_id == 127.0, groups, sender).astype(i32)
    lmult[...] = jnp.where(times > 0.0, jnp.log2(jnp.maximum(times, 1.0)), NONE)

    A[...] = jnp.dot(V[0:BLOCKS, :, 128:256].reshape(NODE, 128), fa[...],
                     preferred_element_type=f32).astype(bf16).reshape(BLOCKS, TILE, 32)
    own_b = jnp.dot(fb[...], rows_s[...].astype(bf16), preferred_element_type=f32).astype(bf16)
    lmass = jnp.log2(mass[...])
    for b in range(BLOCKS):
        B[b] = own_b[:, b * TILE:(b + 1) * TILE]
        lm[b] = lmass[:, b * TILE:(b + 1) * TILE]

    fid = ids[...].astype(f32)
    high = jnp.floor(fid * (1.0 / FR_DEV))
    want[0:1] = high
    want[1:2] = fid - high * FR_DEV
    woff = w_offset[...] * (1.0 / LOG2E)
    wh = woff.astype(bf16).astype(f32)
    wm = woff - wh
    w_in[256:384] = jnp.concatenate(
        [wh, wh, wh, jnp.zeros((7, 128), f32), wm, wm, wm, jnp.zeros((103, 128), f32)], axis=0).astype(bf16)
    w_in[384:512] = jnp.concatenate([wh, wh, wh, jnp.zeros((119, 128), f32)], axis=0).astype(bf16)
    wo = w_out[...].astype(f32)
    wc = wo - jnp.mean(wo, axis=1, keepdims=True)
    wc_h = wc.astype(bf16)
    wc2[0:128] = wc_h
    wc2[128:256] = (wc - wc_h.astype(f32)).astype(bf16)

    row_id = lax.broadcasted_iota(i32, (128, 128), 0)
    mass_map = jnp.where((row_id >= 9) & (row_id < 12), 1.0, 0.0).astype(bf16)
    for b in range(BLOCKS):
        own = V[b, :, 128:256]
        acc[b, :, 0:128] = jnp.zeros((TILE, 128), f32)
        acc[b, :, 128:256] = jnp.dot(own, mass_map, preferred_element_type=f32) * own.astype(f32)

    for pair in ((0, 3), (1, 2)):
        for k in pair:
            o = OFFSETS[k]

            @pl.when((s - o >= 0) & (s - o < n_space))
            def _():
                for c in copies(k):
                    c.wait_recv()

        aux = jnp.concatenate([raux[k] for k in pair], axis=1)
        far_b = jnp.dot(fb[...], aux, preferred_element_type=f32).astype(bf16)
        aux = aux.astype(f32)
        cols = aux_columns(aux).astype(bf16)
        far_mass = aux[9:10] + aux[10:11] + aux[11:12]
        far_lm = jnp.where(far_mass > 0.0, jnp.log2(jnp.maximum(far_mass, 1e-30)), NONE)
        for p, k in enumerate(pair):
            first = BLOCKS + 2 * k
            V[first:first + 2, :, 0:128] = rval[k].reshape(2, TILE, D)
            V[first:first + 2, :, 128:256] = cols[p * HALO:(p + 1) * HALO].reshape(2, TILE, 128)
            for h in range(2):
                at = p * HALO + h * TILE
                B[first + h] = far_b[:, at:at + TILE]
                lm[first + h] = far_lm[:, at:at + TILE]

    for k in range(4):
        o = OFFSETS[k]

        @pl.when((s + o >= 0) & (s + o < n_space))
        def _():
            for c in copies(k):
                c.wait_send()


def tile_kernel(codes, lmult, A, B, V, lm, acc_in, lat, w_in, wc2, rows, acc, upd_h, upd, wb, osem):
    wb[...] = jnp.zeros_like(wb)
    total = lax.fori_loop(0, BLOCKS, lambda r, t: t + codes[r, 127], 0)

    def advance(state):
        out = []
        for _ in range(UNROLL):
            r, g = state
            over = g + 1 >= codes[r, 127]
            state = (jnp.minimum(jnp.where(over, r + 1, r), BLOCKS - 1), jnp.where(over, 0, g + 1))
            out.append(state)
        return out

    def step(it, states):
        now, last = states[:UNROLL], states[UNROLL:]
        def distances(q):
            r, g = now[q]
            pair = jnp.concatenate([B[codes[r, g * GROUP + u]] for u in range(GROUP)], axis=1)
            return jnp.dot(A[r], pair, preferred_element_type=f32)

        ahead = distances(0)
        for q in range(UNROLL):
            r, g = last[q]
            sent = jnp.concatenate([V[codes[r, g * GROUP + u]] for u in range(GROUP)], axis=0)
            acc[r] = acc[r] + jnp.dot(wb[q], sent, preferred_element_type=f32)
            sq = ahead
            if q + 1 < UNROLL:
                ahead = distances(q + 1)
            r, g = now[q]
            off = jnp.where(it * UNROLL + q < total, 0.0, NONE).astype(f32)
            for u in range(GROUP):
                level = lm[codes[r, g * GROUP + u]] + (lmult[r, g * GROUP + u] + off)
                d2 = jnp.maximum(sq[:, u * TILE:(u + 1) * TILE], 1e-12)
                wb[q, :, u * TILE:(u + 1) * TILE] = jnp.exp2(level - d2 * lax.rsqrt(d2)).astype(bf16)
        return tuple(advance(now[-1])) + tuple(now)

    zero = jnp.int32(0)
    first = [(zero, zero)] + advance((zero, zero))[:UNROLL - 1]
    lax.fori_loop(0, (total + UNROLL - 1) // UNROLL + 1, step, tuple(first) + ((zero, zero),) * UNROLL)

    bias_row = rows[0:1]
    gain_row = rows[1:2]
    PIECES = 8
    outs = [pltpu.make_async_copy(upd.at[pl.ds(i * (NODE // PIECES), NODE // PIECES)],
                                  upd_h.at[pl.ds(i * (NODE // PIECES), NODE // PIECES)], osem.at[i])
            for i in range(PIECES)]

    def stage1(b):
        tot = acc[b, :, 128:256]
        rs = lax.rsqrt(tot[:, 12:13])
        agg = (acc[b, :, 0:128] * rs).astype(bf16)
        q = tot * (rs * rs) - V[b, :, 128:256].astype(f32)
        qh = q.astype(bf16)
        qm = (q - qh.astype(f32)).astype(bf16)
        return jnp.concatenate([lat[b * TILE:(b + 1) * TILE], agg, qh, qm], axis=1)

    def stage2(cat):
        pre = jnp.dot(cat, w_in[...], preferred_element_type=f32) + bias_row
        hid = (pre * (0.5 + 0.5 * jnp.tanh(0.5 * pre))).astype(bf16)
        return jnp.concatenate([hid, hid], axis=1)

    def stage3(b, hid):
        cen = jnp.dot(hid, wc2[...], preferred_element_type=f32)
        var = jnp.mean(cen * cen, axis=1, keepdims=True)
        out = lat[b * TILE:(b + 1) * TILE].astype(f32) + cen * lax.rsqrt(var + 1e-5) * gain_row
        upd[b * TILE:(b + 1) * TILE] = out.astype(bf16)

    cats, hids = {}, {}
    for b in range(BLOCKS + 2):
        if b >= 2:
            stage3(b - 2, hids.pop(b - 2))
            if (b - 1) % (BLOCKS // PIECES) == 0:
                outs[(b - 2) // (BLOCKS // PIECES)].start()
        if 1 <= b <= BLOCKS:
            hids[b - 1] = stage2(cats.pop(b - 1))
        if b < BLOCKS:
            cats[b] = stage1(b)
    for c in outs:
        c.wait()


NZ = 8
NY = 4


def pool_kernel(upd, want, out, hot, part, g1, a2, g2, a3, g3, full, s1, r1, s2, r2, s3, r3, s4, r4):
    s = lax.axis_index("space")
    f = lax.axis_index("frag")
    nf = lax.axis_size("frag")
    y = s // NZ
    z = lax.rem(s, NZ)
    barrier = pltpu.get_barrier_semaphore()

    def dev(dy, dz, df):
        return (lax.rem(y + dy, NY) * NZ + lax.rem(z + dz, NZ), lax.rem(f + df, nf))

    peers = [dev(0, 0, i) for i in range(1, nf)] + [dev(i, 0, 0) for i in range(1, NY)]
    peers += [dev(0, i, 0) for i in range(1, NZ)]
    for p in peers:
        pl.semaphore_signal(barrier, inc=1, device_id=p, device_id_type=MESH)

    def remote(src, dst, send, recv, i, to):
        return pltpu.make_async_remote_copy(
            src_ref=src, dst_ref=dst, send_sem=send.at[i - 1], recv_sem=recv.at[i - 1],
            device_id=to, device_id_type=MESH)

    c1 = {i: remote(part.at[i], g1.at[i - 1], s1, r1, i, dev(0, 0, i)) for i in range(1, nf)}
    c2 = {i: remote(a2.at[lax.rem(y + i, NY)], g2.at[i - 1], s2, r2, i, dev(i, 0, 0)) for i in range(1, NY)}
    c3 = {i: remote(a3, g3.at[i - 1], s3, r3, i, dev(0, i, 0)) for i in range(1, NZ)}
    c4 = {i: remote(full.at[y], full.at[y], s4, r4, i, dev(i, 0, 0)) for i in range(1, NY)}

    sub = lax.broadcasted_iota(i32, (FR_DEV, TILE), 0).astype(f32).astype(bf16)
    high = want[0:1]
    low = want[1:2]

    def build(slot, place, i):
        t = lax.rem(f + i, nf).astype(f32)
        row = jnp.where(high == t, low, -1.0).astype(bf16)
        for b in range(BLOCKS):
            cut = jnp.broadcast_to(row[:, b * TILE:(b + 1) * TILE], (FR_DEV, TILE))
            hot[slot, place * FR_DEV:(place + 1) * FR_DEV, b * TILE:(b + 1) * TILE] = jnp.where(
                cut == sub, 1.0, 0.0).astype(bf16)

    order = (4, 3, 5, 2, 6, 1, 7, 0)
    BATCH = 4
    for n in range(BATCH):
        build(0, n, order[n])
    for slot in range(nf // BATCH):
        if slot + 1 < nf // BATCH:
            for n in range(BATCH):
                build(slot + 1, n, order[(slot + 1) * BATCH + n])
        sums = jnp.dot(hot[slot], upd[...], preferred_element_type=f32)
        if slot == 0:
            pl.semaphore_wait(barrier, nf + NY + NZ - 3)
        for n in range(BATCH):
            i = order[slot * BATCH + n]
            mine = sums[n * FR_DEV:(n + 1) * FR_DEV]
            if i:
                part[i] = mine.astype(bf16)
                c1[i].start()
            else:
                total = mine
    for i in order[:-1]:
        c1[i].wait_recv()
        total = total + g1[i - 1].astype(f32)
    a2[...] = total.astype(bf16).reshape(NY, FR_DEV // NY, D)
    for i in (2, 1, 3):
        c2[i].start()
    total = a2[y].astype(f32)
    for i in (1, 3, 2):
        c2[i].wait_recv()
        total = total + g2[i - 1].astype(f32)
    a3[...] = total.astype(bf16)
    for i in (4, 3, 5, 2, 6, 1, 7):
        c3[i].start()
    total = a3[...].astype(f32)
    for i in (1, 7, 2, 6, 3, 5, 4):
        c3[i].wait_recv()
        total = total + g3[i - 1].astype(f32)
    full[y] = total
    for i in (2, 1, 3):
        c4[i].start()
    for i in (1, 3, 2):
        c4[i].wait_recv()
    out[...] = full[...].reshape(FR_DEV, D)
    for group in (c1, c2, c3, c4):
        for c in group.values():
            c.wait_send()


def shards(latents, positions, masses, w_value, w_self, w_message, w_offset, bias_hidden, w_out, norm_gain,
           tile_blocks, tile_count, send_rows, frag_ids):
    ns, nf = lax.axis_size("space"), lax.axis_size("frag")
    vm = pl.BlockSpec(memory_space=pltpu.VMEM)
    sm = pl.BlockSpec(memory_space=pltpu.SMEM)
    hbm = pl.BlockSpec(memory_space=pltpu.HBM)
    fa, fb = feature_maps()
    dma = pltpu.SemaphoreType.DMA
    vmem = pltpu.VMEM
    limit = 36 << 20
    pin = lambda a: pltpu.with_memory_space_constraint(a, pltpu.HBM)
    A, B, V, lm, codes, lmult, acc, lat, w_in, wc2, rows, want = pl.pallas_call(
        halo_kernel,
        out_shape=(
            jax.ShapeDtypeStruct((BLOCKS, TILE, 32), bf16),
            jax.ShapeDtypeStruct((EXT, 32, TILE), bf16),
            jax.ShapeDtypeStruct((EXT, TILE, 256), bf16),
            jax.ShapeDtypeStruct((EXT, 1, TILE), f32),
            jax.ShapeDtypeStruct((BLOCKS, 128), i32),
            jax.ShapeDtypeStruct((BLOCKS, 128), f32),
            jax.ShapeDtypeStruct((BLOCKS, TILE, 256), f32),
            jax.ShapeDtypeStruct((NODE, D), bf16),
            jax.ShapeDtypeStruct((512, D), bf16),
            jax.ShapeDtypeStruct((256, D), bf16),
            jax.ShapeDtypeStruct((2, D), f32),
            jax.ShapeDtypeStruct((2, NODE), f32),
        ),
        in_specs=[hbm] * 5 + [sm] + [hbm] * 10,
        out_specs=(vm,) * 12,
        scratch_shapes=[
            vmem((3, NODE), f32), vmem((1, NODE), f32), vmem((D, D), bf16),
            vmem((2, SLOTS), i32), vmem((4, HALO), i32), vmem((128, 32), bf16), vmem((32, 16), bf16),
            vmem((3, D), f32), vmem((D, D), bf16), vmem((1, NODE), i32),
            vmem((16, NODE), f32),
            vmem((2 * HALO, NODE), bf16),
            vmem((4, HALO, D), bf16),
            vmem((4, 16, HALO), bf16),
            vmem((4, HALO, D), bf16),
            vmem((4, 16, HALO), bf16),
            dma((15,)),
            dma((2, 4)),
            dma((2, 4)),
        ],
        compiler_params=pltpu.CompilerParams(collective_id=0, has_side_effects=True, vmem_limit_bytes=limit),
    )(pin(latents), pin(positions), pin(masses.reshape(1, NODE)), pin(w_value), pin(tile_blocks), tile_count,
      pin(send_rows), pin(fa), pin(fb),
      pin(w_self), pin(w_message), pin(w_offset), pin(bias_hidden.reshape(1, D)), pin(w_out),
      pin(norm_gain.reshape(1, D)),
      pin(frag_ids.reshape(1, NODE)))

    _, updated, upd = pl.pallas_call(
        tile_kernel,
        out_shape=(
            jax.ShapeDtypeStruct((BLOCKS, TILE, 256), f32),
            jax.ShapeDtypeStruct((NODE, D), bf16),
            jax.ShapeDtypeStruct((NODE, D), bf16),
        ),
        in_specs=[sm, sm] + [vm] * 9,
        out_specs=(vm, hbm, vm),
        input_output_aliases={6: 0},
        scratch_shapes=[vmem((UNROLL, TILE, GROUP * TILE), bf16), dma((8,))],
        compiler_params=pltpu.CompilerParams(vmem_limit_bytes=limit),
    )(codes, lmult, A, B, V, lm, acc, lat, w_in, wc2, rows)

    pooled = pl.pallas_call(
        pool_kernel,
        out_shape=jax.ShapeDtypeStruct((FR_DEV, D), f32),
        in_specs=[vm, vm],
        out_specs=vm,
        scratch_shapes=[
            vmem((2, 4 * FR_DEV, NODE), bf16),
            vmem((nf, FR_DEV, D), bf16),
            vmem((nf - 1, FR_DEV, D), bf16),
            vmem((NY, FR_DEV // NY, D), bf16),
            vmem((NY - 1, FR_DEV // NY, D), bf16),
            vmem((FR_DEV // NY, D), bf16),
            vmem((NZ - 1, FR_DEV // NY, D), bf16),
            vmem((NY, FR_DEV // NY, D), f32),
            dma((nf - 1,)), dma((nf - 1,)),
            dma((NY - 1,)), dma((NY - 1,)),
            dma((NZ - 1,)), dma((NZ - 1,)),
            dma((NY - 1,)), dma((NY - 1,)),
        ],
        compiler_params=pltpu.CompilerParams(collective_id=1, has_side_effects=True, vmem_limit_bytes=limit),
    )(upd, want)
    return updated, pooled * math.sqrt(FR_DEV * nf / (NODE * ns * nf))


def solution(mesh):
    own = P(("space", "frag"))
    return jax.shard_map(
        shards,
        mesh=mesh,
        in_specs=(
            P(("space", "frag"), None), P(None, ("space", "frag")), own,
            P(), P(), P(), P(), P(), P(), P(),
            P(None, ("space", "frag")), own, P(None, ("space", "frag")), own,
        ),
        out_specs=(P(("space", "frag"), None), P("frag", None)),
        check_vma=False,
    )
```

```python
import math

import jax
import jax.numpy as jnp
import numpy as np
from jax import lax
from jax.experimental import pallas as pl
from jax.experimental.pallas import tpu as pltpu
from jax.sharding import PartitionSpec as P

D = 128
TILE = 128
REACH = 2
HALO = 256
BLOCKS = 32
EXT = 40
NODE = BLOCKS * TILE
SLOTS = 640
FR_DEV = 128
OFFSETS = tuple(o for o in range(-REACH, REACH + 1) if o != 0)
LOG2E = math.log2(math.e)
CENTRE = 6.0
GROUP = 2
UNROLL = 16
NONE = -1e30

f32, bf16, i32 = jnp.float32, jnp.bfloat16, jnp.int32
MESH = pl.DeviceIdType.MESH


def split3(x):
    high = x.astype(bf16).astype(f32)
    rest = x - high
    mid = rest.astype(bf16).astype(f32)
    return high, mid, rest - mid


def feature_maps():
    recv = np.zeros((128, 32), np.float32)
    send = np.zeros((32, 16), np.float32)
    pairs = ((0, 0), (0, 1), (1, 0), (1, 1), (0, 2), (2, 0))
    for p, (a, b) in enumerate(pairs):
        for c in range(3):
            recv[3 * a + c, 3 * p + c] = -2.0
            send[3 * p + c, 3 * b + c] = 1.0
    for c in range(3):
        recv[13 + c, 18 + c] = 1.0
        send[18 + c, 12] = 1.0
        recv[12, 21 + c] = 1.0
        send[21 + c, 13 + c] = 1.0
    return jnp.asarray(recv, bf16), jnp.asarray(send, bf16)


def aux_columns(rows):
    cols = jnp.transpose(jnp.concatenate([rows, rows], axis=0))
    return jnp.concatenate([cols, jnp.zeros((cols.shape[0], 96), f32)], axis=1)


def halo_kernel(lat_h, pos_h, mass_h, wv_h, tb_h, tc, sr_h, fa_h, fb_h,
                ws_h, wmsg_h, woff_h, bias_h, wo_h, gain_h, ids_h,
                A, B, V, lm, codes, lmult, acc, lat, w_in, wc2, rows_out, want,
                pos, mass, wv, tb, sr, fa, fb, w_offset, w_out, ids,
                rows_s, hot, sval, saux, rval, raux, isem, ssem, rsem):
    s = lax.axis_index("space")
    f = lax.axis_index("frag")
    n_space = lax.axis_size("space")
    loads = [pltpu.make_async_copy(src, dst, isem.at[i]) for i, (src, dst) in enumerate((
        (sr_h, sr), (pos_h, pos), (mass_h, mass), (lat_h, lat), (wv_h, wv), (tb_h, tb), (fa_h, fa), (fb_h, fb),
        (ws_h, w_in.at[0:128]), (wmsg_h, w_in.at[128:256]), (woff_h, w_offset), (wo_h, w_out),
        (bias_h, rows_out.at[0:1]), (gain_h, rows_out.at[1:2]), (ids_h, ids)))]
    for c in loads:
        c.start()
    barrier = pltpu.get_barrier_semaphore()
    for o in OFFSETS:
        @pl.when((s + o >= 0) & (s + o < n_space))
        def _():
            pl.semaphore_signal(barrier, inc=1, device_id=(s + o, f), device_id_type=MESH)

    loads[1].wait()
    loads[2].wait()
    x = (pos[...] - CENTRE) * LOG2E
    xh, xm, xl = split3(x)
    mh, mm, ml = split3(mass[...])
    sq = x * x
    norm = sq[0:1] + sq[1:2] + sq[2:3]
    nh, nm, nl = split3(norm)
    rows_s[...] = jnp.concatenate([xh, xm, xl, mh, mm, ml, jnp.ones((1, NODE), f32), nh, nm, nl], axis=0)
    for b in range(BLOCKS):
        V[b, :, 128:256] = aux_columns(rows_s[:, b * TILE:(b + 1) * TILE]).astype(bf16)
    loads[3].wait()
    loads[4].wait()
    loads[0].wait()
    values = jnp.dot(lat[...], wv[...], preferred_element_type=f32).astype(bf16)
    V[0:BLOCKS, :, 0:128] = values.reshape(BLOCKS, TILE, D)

    def copies(k):
        o = OFFSETS[k]
        dev = (s + o, f)
        return (
            pltpu.make_async_remote_copy(
                src_ref=sval.at[k], dst_ref=rval.at[k], send_sem=ssem.at[0, k], recv_sem=rsem.at[0, k],
                device_id=dev, device_id_type=MESH),
            pltpu.make_async_remote_copy(
                src_ref=saux.at[k], dst_ref=raux.at[k], send_sem=ssem.at[1, k], recv_sem=rsem.at[1, k],
                device_id=dev, device_id_type=MESH),
        )

    idx = sr[...].astype(f32)
    idx = jnp.transpose(jnp.concatenate([idx, idx], axis=0))
    lane = lax.broadcasted_iota(i32, (HALO, TILE), 1).astype(f32)
    for first, pair in ((True, (0, 3)), (False, (1, 2))):
        for p, k in enumerate(pair):
            col = idx[:, k:k + 1]
            high = jnp.floor(col * (1.0 / TILE))
            low = col - high * TILE
            code = jnp.where(low == lane, high, -1.0).astype(bf16)
            for b in range(BLOCKS):
                hot[p * HALO:(p + 1) * HALO, b * TILE:(b + 1) * TILE] = jnp.where(
                    code == jnp.asarray(b, bf16), 1.0, 0.0).astype(bf16)
        got = jnp.dot(hot[...], V[0:BLOCKS].reshape(NODE, 256), preferred_element_type=f32)
        if first:
            pl.semaphore_wait(barrier, jnp.minimum(s, REACH) + jnp.minimum(n_space - 1 - s, REACH))
        for p, k in enumerate(pair):
            part = got[p * HALO:(p + 1) * HALO]
            sval[k] = part[:, 0:128].astype(bf16)
            saux[k] = jnp.transpose(part[:, 128:256])[0:16].astype(bf16)
            o = OFFSETS[k]

            @pl.when((s + o >= 0) & (s + o < n_space))
            def _():
                for c in copies(k):
                    c.start()

            @pl.when((s - o < 0) | (s - o >= n_space))
            def _():
                rval[k] = jnp.zeros((HALO, D), bf16)
                raux[k] = jnp.zeros((16, HALO), bf16)

    for c in loads[5:]:
        c.wait()
    slot = lax.broadcasted_iota(i32, (BLOCKS, SLOTS), 1)
    rhot = (lax.broadcasted_iota(i32, (BLOCKS, SLOTS), 0) == tb[0:1, :]) & (slot < tc[0])
    chot = lax.broadcasted_iota(i32, (128, SLOTS), 0) == tb[1:2, :]
    count = lax.dot_general(
        jnp.where(rhot, 1.0, 0.0).astype(bf16), jnp.where(chot, 1.0, 0.0).astype(bf16),
        (((1,), (1,)), ((), ())), preferred_element_type=f32)
    live = jnp.where(count > 0.0, 1.0, 0.0)
    before = lax.broadcasted_iota(i32, (128, 128), 0) < lax.broadcasted_iota(i32, (128, 128), 1)
    place = jnp.dot(live.astype(bf16), jnp.where(before, 1.0, 0.0).astype(bf16), preferred_element_type=f32)
    place = jnp.where(count > 0.0, place, -1.0)
    col_id = lax.broadcasted_iota(i32, (BLOCKS, 128), 1).astype(f32)
    packed = col_id + 64.0 * count
    listed = jnp.zeros((BLOCKS, 128), f32)
    for c in range(EXT):
        listed = listed + jnp.where(place[:, c:c + 1] == col_id, packed[:, c:c + 1], 0.0)
    times = jnp.floor(listed * (1.0 / 64.0))
    sender = listed - 64.0 * times
    groups = jnp.maximum(jnp.floor((jnp.sum(live, axis=1, keepdims=True) + (GROUP - 1)) * (1.0 / GROUP)), 1.0)
    codes[...] = jnp.where(col_id == 127.0, groups, sender).astype(i32)
    lmult[...] = jnp.where(times > 0.0, jnp.log2(jnp.maximum(times, 1.0)), NONE)

    A[...] = jnp.dot(V[0:BLOCKS, :, 128:256].reshape(NODE, 128), fa[...],
                     preferred_element_type=f32).astype(bf16).reshape(BLOCKS, TILE, 32)
    own_b = jnp.dot(fb[...], rows_s[...].astype(bf16), preferred_element_type=f32).astype(bf16)
    lmass = jnp.log2(mass[...])
    for b in range(BLOCKS):
        B[b] = own_b[:, b * TILE:(b + 1) * TILE]
        lm[b] = lmass[:, b * TILE:(b + 1) * TILE]

    fid = ids[...].astype(f32)
    high = jnp.floor(fid * (1.0 / FR_DEV))
    want[0:1] = high
    want[1:2] = fid - high * FR_DEV
    woff = w_offset[...] * (1.0 / LOG2E)
    wh = woff.astype(bf16).astype(f32)
    wm = woff - wh
    w_in[256:384] = jnp.concatenate(
        [wh, wh, wh, jnp.zeros((7, 128), f32), wm, wm, wm, jnp.zeros((103, 128), f32)], axis=0).astype(bf16)
    w_in[384:512] = jnp.concatenate([wh, wh, wh, jnp.zeros((119, 128), f32)], axis=0).astype(bf16)
    wo = w_out[...].astype(f32)
    wc = wo - jnp.mean(wo, axis=1, keepdims=True)
    wc_h = wc.astype(bf16)
    wc2[0:128] = wc_h
    wc2[128:256] = (wc - wc_h.astype(f32)).astype(bf16)

    row_id = lax.broadcasted_iota(i32, (128, 128), 0)
    mass_map = jnp.where((row_id >= 9) & (row_id < 12), 1.0, 0.0).astype(bf16)
    for b in range(BLOCKS):
        own = V[b, :, 128:256]
        acc[b, :, 0:128] = jnp.zeros((TILE, 128), f32)
        acc[b, :, 128:256] = jnp.dot(own, mass_map, preferred_element_type=f32) * own.astype(f32)

    for pair in ((0, 3), (1, 2)):
        for k in pair:
            o = OFFSETS[k]

            @pl.when((s - o >= 0) & (s - o < n_space))
            def _():
                for c in copies(k):
                    c.wait_recv()

        aux = jnp.concatenate([raux[k] for k in pair], axis=1)
        far_b = jnp.dot(fb[...], aux, preferred_element_type=f32).astype(bf16)
        aux = aux.astype(f32)
        cols = aux_columns(aux).astype(bf16)
        far_mass = aux[9:10] + aux[10:11] + aux[11:12]
        far_lm = jnp.where(far_mass > 0.0, jnp.log2(jnp.maximum(far_mass, 1e-30)), NONE)
        for p, k in enumerate(pair):
            first = BLOCKS + 2 * k
            V[first:first + 2, :, 0:128] = rval[k].reshape(2, TILE, D)
            V[first:first + 2, :, 128:256] = cols[p * HALO:(p + 1) * HALO].reshape(2, TILE, 128)
            for h in range(2):
                at = p * HALO + h * TILE
                B[first + h] = far_b[:, at:at + TILE]
                lm[first + h] = far_lm[:, at:at + TILE]

    for k in range(4):
        o = OFFSETS[k]

        @pl.when((s + o >= 0) & (s + o < n_space))
        def _():
            for c in copies(k):
                c.wait_send()


def tile_kernel(codes, lmult, A, B, V, lm, acc_in, lat, w_in, wc2, rows, acc, upd_h, upd, wb, osem):
    wb[...] = jnp.zeros_like(wb)
    total = lax.fori_loop(0, BLOCKS, lambda r, t: t + codes[r, 127], 0)

    def advance(state):
        out = []
        for _ in range(UNROLL):
            r, g = state
            over = g + 1 >= codes[r, 127]
            state = (jnp.minimum(jnp.where(over, r + 1, r), BLOCKS - 1), jnp.where(over, 0, g + 1))
            out.append(state)
        return out

    def step(it, states):
        now, last = states[:UNROLL], states[UNROLL:]
        def distances(q):
            r, g = now[q]
            pair = jnp.concatenate([B[codes[r, g * GROUP + u]] for u in range(GROUP)], axis=1)
            return jnp.dot(A[r], pair, preferred_element_type=f32)

        ahead = distances(0)
        for q in range(UNROLL):
            r, g = last[q]
            sent = jnp.concatenate([V[codes[r, g * GROUP + u]] for u in range(GROUP)], axis=0)
            acc[r] = acc[r] + jnp.dot(wb[q], sent, preferred_element_type=f32)
            sq = ahead
            if q + 1 < UNROLL:
                ahead = distances(q + 1)
            r, g = now[q]
            off = jnp.where(it * UNROLL + q < total, 0.0, NONE).astype(f32)
            for u in range(GROUP):
                level = lm[codes[r, g * GROUP + u]] + (lmult[r, g * GROUP + u] + off)
                d2 = jnp.maximum(sq[:, u * TILE:(u + 1) * TILE], 1e-12)
                wb[q, :, u * TILE:(u + 1) * TILE] = jnp.exp2(level - d2 * lax.rsqrt(d2)).astype(bf16)
        return tuple(advance(now[-1])) + tuple(now)

    zero = jnp.int32(0)
    first = [(zero, zero)] + advance((zero, zero))[:UNROLL - 1]
    lax.fori_loop(0, (total + UNROLL - 1) // UNROLL + 1, step, tuple(first) + ((zero, zero),) * UNROLL)

    bias_row = rows[0:1]
    gain_row = rows[1:2]
    PIECES = 8
    outs = [pltpu.make_async_copy(upd.at[pl.ds(i * (NODE // PIECES), NODE // PIECES)],
                                  upd_h.at[pl.ds(i * (NODE // PIECES), NODE // PIECES)], osem.at[i])
            for i in range(PIECES)]

    STEP = 2
    PARTS = BLOCKS // STEP

    def rows_of(p):
        return slice(p * STEP * TILE, (p + 1) * STEP * TILE)

    def stage1(p):
        got = acc[p * STEP:(p + 1) * STEP].reshape(STEP * TILE, 256)
        tot = got[:, 128:256]
        rs = lax.rsqrt(tot[:, 12:13])
        agg = (got[:, 0:128] * rs).astype(bf16)
        own = V[p * STEP:(p + 1) * STEP, :, 128:256].reshape(STEP * TILE, 128).astype(f32)
        q = tot * (rs * rs) - own
        qh = q.astype(bf16)
        qm = (q - qh.astype(f32)).astype(bf16)
        return jnp.concatenate([lat[rows_of(p)], agg, qh, qm], axis=1)

    def stage2(cat):
        pre = jnp.dot(cat, w_in[...], preferred_element_type=f32) + bias_row
        hid = (pre * (0.5 + 0.5 * jnp.tanh(0.5 * pre))).astype(bf16)
        return jnp.concatenate([hid, hid], axis=1)

    def stage3(p, hid):
        cen = jnp.dot(hid, wc2[...], preferred_element_type=f32)
        var = jnp.mean(cen * cen, axis=1, keepdims=True)
        out = lat[rows_of(p)].astype(f32) + cen * lax.rsqrt(var + 1e-5) * gain_row
        upd[rows_of(p)] = out.astype(bf16)

    cats, hids = {}, {}
    for p in range(PARTS + 2):
        if p >= 2:
            stage3(p - 2, hids.pop(p - 2))
            if (p - 1) % (PARTS // PIECES) == 0:
                outs[(p - 2) // (PARTS // PIECES)].start()
        if 1 <= p <= PARTS:
            hids[p - 1] = stage2(cats.pop(p - 1))
        if p < PARTS:
            cats[p] = stage1(p)
    for c in outs:
        c.wait()


NZ = 8
NY = 4


def pool_kernel(upd, want, out, hot, part, g1, a2, g2, a3, g3, full, s1, r1, s2, r2, s3, r3, s4, r4):
    s = lax.axis_index("space")
    f = lax.axis_index("frag")
    nf = lax.axis_size("frag")
    y = s // NZ
    z = lax.rem(s, NZ)
    barrier = pltpu.get_barrier_semaphore()

    def dev(dy, dz, df):
        return (lax.rem(y + dy, NY) * NZ + lax.rem(z + dz, NZ), lax.rem(f + df, nf))

    peers = [dev(0, 0, i) for i in range(1, nf)] + [dev(i, 0, 0) for i in range(1, NY)]
    peers += [dev(0, i, 0) for i in range(1, NZ)]
    for p in peers:
        pl.semaphore_signal(barrier, inc=1, device_id=p, device_id_type=MESH)

    def remote(src, dst, send, recv, i, to):
        return pltpu.make_async_remote_copy(
            src_ref=src, dst_ref=dst, send_sem=send.at[i - 1], recv_sem=recv.at[i - 1],
            device_id=to, device_id_type=MESH)

    c1 = {i: remote(part.at[i], g1.at[i - 1], s1, r1, i, dev(0, 0, i)) for i in range(1, nf)}
    c2 = {i: remote(a2.at[lax.rem(y + i, NY)], g2.at[i - 1], s2, r2, i, dev(i, 0, 0)) for i in range(1, NY)}
    c3 = {i: remote(a3, g3.at[i - 1], s3, r3, i, dev(0, i, 0)) for i in range(1, NZ)}
    c4 = {i: remote(full.at[y], full.at[y], s4, r4, i, dev(i, 0, 0)) for i in range(1, NY)}

    sub = lax.broadcasted_iota(i32, (FR_DEV, TILE), 0).astype(f32).astype(bf16)
    high = want[0:1]
    low = want[1:2]

    def build(slot, place, i):
        t = lax.rem(f + i, nf).astype(f32)
        row = jnp.where(high == t, low, -1.0).astype(bf16)
        for b in range(BLOCKS):
            cut = jnp.broadcast_to(row[:, b * TILE:(b + 1) * TILE], (FR_DEV, TILE))
            hot[slot, place * FR_DEV:(place + 1) * FR_DEV, b * TILE:(b + 1) * TILE] = jnp.where(
                cut == sub, 1.0, 0.0).astype(bf16)

    order = (4, 3, 5, 2, 6, 1, 7, 0)
    BATCH = 4
    for n in range(BATCH):
        build(0, n, order[n])
    for slot in range(nf // BATCH):
        if slot + 1 < nf // BATCH:
            for n in range(BATCH):
                build(slot + 1, n, order[(slot + 1) * BATCH + n])
        sums = jnp.dot(hot[slot], upd[...], preferred_element_type=f32)
        if slot == 0:
            pl.semaphore_wait(barrier, nf + NY + NZ - 3)
        for n in range(BATCH):
            i = order[slot * BATCH + n]
            mine = sums[n * FR_DEV:(n + 1) * FR_DEV]
            if i:
                part[i] = mine.astype(bf16)
                c1[i].start()
            else:
                total = mine
    for i in order[:-1]:
        c1[i].wait_recv()
        total = total + g1[i - 1].astype(f32)
    a2[...] = total.astype(bf16).reshape(NY, FR_DEV // NY, D)
    for i in (2, 1, 3):
        c2[i].start()
    total = a2[y].astype(f32)
    for i in (1, 3, 2):
        c2[i].wait_recv()
        total = total + g2[i - 1].astype(f32)
    a3[...] = total.astype(bf16)
    for i in (4, 3, 5, 2, 6, 1, 7):
        c3[i].start()
    total = a3[...].astype(f32)
    for i in (1, 7, 2, 6, 3, 5, 4):
        c3[i].wait_recv()
        total = total + g3[i - 1].astype(f32)
    full[y] = total
    for i in (2, 1, 3):
        c4[i].start()
    for i in (1, 3, 2):
        c4[i].wait_recv()
    out[...] = full[...].reshape(FR_DEV, D)
    for group in (c1, c2, c3, c4):
        for c in group.values():
            c.wait_send()


def shards(latents, positions, masses, w_value, w_self, w_message, w_offset, bias_hidden, w_out, norm_gain,
           tile_blocks, tile_count, send_rows, frag_ids):
    ns, nf = lax.axis_size("space"), lax.axis_size("frag")
    vm = pl.BlockSpec(memory_space=pltpu.VMEM)
    sm = pl.BlockSpec(memory_space=pltpu.SMEM)
    hbm = pl.BlockSpec(memory_space=pltpu.HBM)
    fa, fb = feature_maps()
    dma = pltpu.SemaphoreType.DMA
    vmem = pltpu.VMEM
    limit = 36 << 20
    pin = lambda a: pltpu.with_memory_space_constraint(a, pltpu.HBM)
    A, B, V, lm, codes, lmult, acc, lat, w_in, wc2, rows, want = pl.pallas_call(
        halo_kernel,
        out_shape=(
            jax.ShapeDtypeStruct((BLOCKS, TILE, 32), bf16),
            jax.ShapeDtypeStruct((EXT, 32, TILE), bf16),
            jax.ShapeDtypeStruct((EXT, TILE, 256), bf16),
            jax.ShapeDtypeStruct((EXT, 1, TILE), f32),
            jax.ShapeDtypeStruct((BLOCKS, 128), i32),
            jax.ShapeDtypeStruct((BLOCKS, 128), f32),
            jax.ShapeDtypeStruct((BLOCKS, TILE, 256), f32),
            jax.ShapeDtypeStruct((NODE, D), bf16),
            jax.ShapeDtypeStruct((512, D), bf16),
            jax.ShapeDtypeStruct((256, D), bf16),
            jax.ShapeDtypeStruct((2, D), f32),
            jax.ShapeDtypeStruct((2, NODE), f32),
        ),
        in_specs=[hbm] * 5 + [sm] + [hbm] * 10,
        out_specs=(vm,) * 12,
        scratch_shapes=[
            vmem((3, NODE), f32), vmem((1, NODE), f32), vmem((D, D), bf16),
            vmem((2, SLOTS), i32), vmem((4, HALO), i32), vmem((128, 32), bf16), vmem((32, 16), bf16),
            vmem((3, D), f32), vmem((D, D), bf16), vmem((1, NODE), i32),
            vmem((16, NODE), f32),
            vmem((2 * HALO, NODE), bf16),
            vmem((4, HALO, D), bf16),
            vmem((4, 16, HALO), bf16),
            vmem((4, HALO, D), bf16),
            vmem((4, 16, HALO), bf16),
            dma((15,)),
            dma((2, 4)),
            dma((2, 4)),
        ],
        compiler_params=pltpu.CompilerParams(collective_id=0, has_side_effects=True, vmem_limit_bytes=limit),
    )(pin(latents), pin(positions), pin(masses.reshape(1, NODE)), pin(w_value), pin(tile_blocks), tile_count,
      pin(send_rows), pin(fa), pin(fb),
      pin(w_self), pin(w_message), pin(w_offset), pin(bias_hidden.reshape(1, D)), pin(w_out),
      pin(norm_gain.reshape(1, D)),
      pin(frag_ids.reshape(1, NODE)))

    _, updated, upd = pl.pallas_call(
        tile_kernel,
        out_shape=(
            jax.ShapeDtypeStruct((BLOCKS, TILE, 256), f32),
            jax.ShapeDtypeStruct((NODE, D), bf16),
            jax.ShapeDtypeStruct((NODE, D), bf16),
        ),
        in_specs=[sm, sm] + [vm] * 9,
        out_specs=(vm, hbm, vm),
        input_output_aliases={6: 0},
        scratch_shapes=[vmem((UNROLL, TILE, GROUP * TILE), bf16), dma((8,))],
        compiler_params=pltpu.CompilerParams(vmem_limit_bytes=limit),
    )(codes, lmult, A, B, V, lm, acc, lat, w_in, wc2, rows)

    pooled = pl.pallas_call(
        pool_kernel,
        out_shape=jax.ShapeDtypeStruct((FR_DEV, D), f32),
        in_specs=[vm, vm],
        out_specs=vm,
        scratch_shapes=[
            vmem((2, 4 * FR_DEV, NODE), bf16),
            vmem((nf, FR_DEV, D), bf16),
            vmem((nf - 1, FR_DEV, D), bf16),
            vmem((NY, FR_DEV // NY, D), bf16),
            vmem((NY - 1, FR_DEV // NY, D), bf16),
            vmem((FR_DEV // NY, D), bf16),
            vmem((NZ - 1, FR_DEV // NY, D), bf16),
            vmem((NY, FR_DEV // NY, D), f32),
            dma((nf - 1,)), dma((nf - 1,)),
            dma((NY - 1,)), dma((NY - 1,)),
            dma((NZ - 1,)), dma((NZ - 1,)),
            dma((NY - 1,)), dma((NY - 1,)),
        ],
        compiler_params=pltpu.CompilerParams(collective_id=1, has_side_effects=True, vmem_limit_bytes=limit),
    )(upd, want)
    return updated, pooled * math.sqrt(FR_DEV * nf / (NODE * ns * nf))


def solution(mesh):
    own = P(("space", "frag"))
    return jax.shard_map(
        shards,
        mesh=mesh,
        in_specs=(
            P(("space", "frag"), None), P(None, ("space", "frag")), own,
            P(), P(), P(), P(), P(), P(), P(),
            P(None, ("space", "frag")), own, P(None, ("space", "frag")), own,
        ),
        out_specs=(P(("space", "frag"), None), P("frag", None)),
        check_vma=False,
    )
```

```python
import math

import jax
import jax.numpy as jnp
import numpy as np
from jax import lax
from jax.experimental import pallas as pl
from jax.experimental.pallas import tpu as pltpu
from jax.sharding import PartitionSpec as P

D = 128
TILE = 128
REACH = 2
HALO = 256
BLOCKS = 32
EXT = 40
NODE = BLOCKS * TILE
SLOTS = 640
FR_DEV = 128
OFFSETS = tuple(o for o in range(-REACH, REACH + 1) if o != 0)
LOG2E = math.log2(math.e)
CENTRE = 6.0
GROUP = 2
UNROLL = 16
NONE = -1e30

f32, bf16, i32 = jnp.float32, jnp.bfloat16, jnp.int32
MESH = pl.DeviceIdType.MESH


def split3(x):
    high = x.astype(bf16).astype(f32)
    rest = x - high
    mid = rest.astype(bf16).astype(f32)
    return high, mid, rest - mid


def feature_maps():
    recv = np.zeros((128, 32), np.float32)
    send = np.zeros((32, 16), np.float32)
    pairs = ((0, 0), (0, 1), (1, 0), (1, 1), (0, 2), (2, 0))
    for p, (a, b) in enumerate(pairs):
        for c in range(3):
            recv[3 * a + c, 3 * p + c] = -2.0
            send[3 * p + c, 3 * b + c] = 1.0
    for c in range(3):
        recv[13 + c, 18 + c] = 1.0
        send[18 + c, 12] = 1.0
        recv[12, 21 + c] = 1.0
        send[21 + c, 13 + c] = 1.0
    return jnp.asarray(recv, bf16), jnp.asarray(send, bf16)


def aux_columns(rows):
    cols = jnp.transpose(jnp.concatenate([rows, rows], axis=0))
    return jnp.concatenate([cols, jnp.zeros((cols.shape[0], 96), f32)], axis=1)


def halo_kernel(lat_h, pos_h, mass_h, wv_h, tb_h, tc, sr_h, fa_h, fb_h,
                ws_h, wmsg_h, woff_h, bias_h, wo_h, gain_h, ids_h,
                A, B, V, lm, codes, lmult, acc, lat, w_in, wc2, rows_out, want,
                pos, mass, wv, tb, sr, fa, fb, w_offset, w_out, ids,
                rows_s, hot, sval, saux, rval, raux, isem, ssem, rsem):
    s = lax.axis_index("space")
    f = lax.axis_index("frag")
    n_space = lax.axis_size("space")
    loads = [pltpu.make_async_copy(src, dst, isem.at[i]) for i, (src, dst) in enumerate((
        (sr_h, sr), (pos_h, pos), (mass_h, mass), (lat_h, lat), (wv_h, wv), (tb_h, tb), (fa_h, fa), (fb_h, fb),
        (ws_h, w_in.at[0:128]), (wmsg_h, w_in.at[128:256]), (woff_h, w_offset), (wo_h, w_out),
        (bias_h, rows_out.at[0:1]), (gain_h, rows_out.at[1:2]), (ids_h, ids)))]
    for c in loads:
        c.start()
    barrier = pltpu.get_barrier_semaphore()
    for o in OFFSETS:
        @pl.when((s + o >= 0) & (s + o < n_space))
        def _():
            pl.semaphore_signal(barrier, inc=1, device_id=(s + o, f), device_id_type=MESH)

    loads[1].wait()
    loads[2].wait()
    x = (pos[...] - CENTRE) * LOG2E
    xh, xm, xl = split3(x)
    mh, mm, ml = split3(mass[...])
    sq = x * x
    norm = sq[0:1] + sq[1:2] + sq[2:3]
    nh, nm, nl = split3(norm)
    rows_s[...] = jnp.concatenate([xh, xm, xl, mh, mm, ml, jnp.ones((1, NODE), f32), nh, nm, nl], axis=0)
    for b in range(BLOCKS):
        V[b, :, 128:256] = aux_columns(rows_s[:, b * TILE:(b + 1) * TILE]).astype(bf16)
    loads[3].wait()
    loads[4].wait()
    loads[0].wait()
    values = jnp.dot(lat[...], wv[...], preferred_element_type=f32).astype(bf16)
    V[0:BLOCKS, :, 0:128] = values.reshape(BLOCKS, TILE, D)

    def copies(k):
        o = OFFSETS[k]
        dev = (s + o, f)
        return (
            pltpu.make_async_remote_copy(
                src_ref=sval.at[k], dst_ref=rval.at[k], send_sem=ssem.at[0, k], recv_sem=rsem.at[0, k],
                device_id=dev, device_id_type=MESH),
            pltpu.make_async_remote_copy(
                src_ref=saux.at[k], dst_ref=raux.at[k], send_sem=ssem.at[1, k], recv_sem=rsem.at[1, k],
                device_id=dev, device_id_type=MESH),
        )

    idx = sr[...].astype(f32)
    idx = jnp.transpose(jnp.concatenate([idx, idx], axis=0))
    lane = lax.broadcasted_iota(i32, (HALO, TILE), 1).astype(f32)
    for first, pair in ((True, (0,)), (False, (3,)), (False, (1,)), (False, (2,))):
        for p, k in enumerate(pair):
            col = idx[:, k:k + 1]
            high = jnp.floor(col * (1.0 / TILE))
            low = col - high * TILE
            code = jnp.where(low == lane, high, -1.0).astype(bf16)
            for b in range(BLOCKS):
                hot[p * HALO:(p + 1) * HALO, b * TILE:(b + 1) * TILE] = jnp.where(
                    code == jnp.asarray(b, bf16), 1.0, 0.0).astype(bf16)
        got = jnp.dot(hot[...], V[0:BLOCKS].reshape(NODE, 256), preferred_element_type=f32)
        if first:
            pl.semaphore_wait(barrier, jnp.minimum(s, REACH) + jnp.minimum(n_space - 1 - s, REACH))
        for p, k in enumerate(pair):
            part = got[p * HALO:(p + 1) * HALO]
            sval[k] = part[:, 0:128].astype(bf16)
            saux[k] = jnp.transpose(part[:, 128:256])[0:16].astype(bf16)
            o = OFFSETS[k]

            @pl.when((s + o >= 0) & (s + o < n_space))
            def _():
                for c in copies(k):
                    c.start()

            @pl.when((s - o < 0) | (s - o >= n_space))
            def _():
                rval[k] = jnp.zeros((HALO, D), bf16)
                raux[k] = jnp.zeros((16, HALO), bf16)

    for c in loads[5:]:
        c.wait()
    slot = lax.broadcasted_iota(i32, (BLOCKS, SLOTS), 1)
    rhot = (lax.broadcasted_iota(i32, (BLOCKS, SLOTS), 0) == tb[0:1, :]) & (slot < tc[0])
    chot = lax.broadcasted_iota(i32, (128, SLOTS), 0) == tb[1:2, :]
    count = lax.dot_general(
        jnp.where(rhot, 1.0, 0.0).astype(bf16), jnp.where(chot, 1.0, 0.0).astype(bf16),
        (((1,), (1,)), ((), ())), preferred_element_type=f32)
    live = jnp.where(count > 0.0, 1.0, 0.0)
    before = lax.broadcasted_iota(i32, (128, 128), 0) < lax.broadcasted_iota(i32, (128, 128), 1)
    place = jnp.dot(live.astype(bf16), jnp.where(before, 1.0, 0.0).astype(bf16), preferred_element_type=f32)
    place = jnp.where(count > 0.0, place, -1.0)
    col_id = lax.broadcasted_iota(i32, (BLOCKS, 128), 1).astype(f32)
    packed = col_id + 64.0 * count
    listed = jnp.zeros((BLOCKS, 128), f32)
    for c in range(EXT):
        listed = listed + jnp.where(place[:, c:c + 1] == col_id, packed[:, c:c + 1], 0.0)
    times = jnp.floor(listed * (1.0 / 64.0))
    sender = listed - 64.0 * times
    groups = jnp.maximum(jnp.floor((jnp.sum(live, axis=1, keepdims=True) + (GROUP - 1)) * (1.0 / GROUP)), 1.0)
    codes[...] = jnp.where(col_id == 127.0, groups, sender).astype(i32)
    lmult[...] = jnp.where(times > 0.0, jnp.log2(jnp.maximum(times, 1.0)), NONE)

    A[...] = jnp.dot(V[0:BLOCKS, :, 128:256].reshape(NODE, 128), fa[...],
                     preferred_element_type=f32).astype(bf16).reshape(BLOCKS, TILE, 32)
    own_b = jnp.dot(fb[...], rows_s[...].astype(bf16), preferred_element_type=f32).astype(bf16)
    lmass = jnp.log2(mass[...])
    for b in range(BLOCKS):
        B[b] = own_b[:, b * TILE:(b + 1) * TILE]
        lm[b] = lmass[:, b * TILE:(b + 1) * TILE]

    fid = ids[...].astype(f32)
    high = jnp.floor(fid * (1.0 / FR_DEV))
    want[0:1] = high
    want[1:2] = fid - high * FR_DEV
    woff = w_offset[...] * (1.0 / LOG2E)
    wh = woff.astype(bf16).astype(f32)
    wm = woff - wh
    w_in[256:384] = jnp.concatenate(
        [wh, wh, wh, jnp.zeros((7, 128), f32), wm, wm, wm, jnp.zeros((103, 128), f32)], axis=0).astype(bf16)
    w_in[384:512] = jnp.concatenate([wh, wh, wh, jnp.zeros((119, 128), f32)], axis=0).astype(bf16)
    wo = w_out[...].astype(f32)
    wc = wo - jnp.mean(wo, axis=1, keepdims=True)
    wc_h = wc.astype(bf16)
    wc2[0:128] = wc_h
    wc2[128:256] = (wc - wc_h.astype(f32)).astype(bf16)

    row_id = lax.broadcasted_iota(i32, (128, 128), 0)
    mass_map = jnp.where((row_id >= 9) & (row_id < 12), 1.0, 0.0).astype(bf16)
    for b in range(BLOCKS):
        own = V[b, :, 128:256]
        acc[b, :, 0:128] = jnp.zeros((TILE, 128), f32)
        acc[b, :, 128:256] = jnp.dot(own, mass_map, preferred_element_type=f32) * own.astype(f32)

    for pair in ((0, 3), (1, 2)):
        for k in pair:
            o = OFFSETS[k]

            @pl.when((s - o >= 0) & (s - o < n_space))
            def _():
                for c in copies(k):
                    c.wait_recv()

        aux = jnp.concatenate([raux[k] for k in pair], axis=1)
        far_b = jnp.dot(fb[...], aux, preferred_element_type=f32).astype(bf16)
        aux = aux.astype(f32)
        cols = aux_columns(aux).astype(bf16)
        far_mass = aux[9:10] + aux[10:11] + aux[11:12]
        far_lm = jnp.where(far_mass > 0.0, jnp.log2(jnp.maximum(far_mass, 1e-30)), NONE)
        for p, k in enumerate(pair):
            first = BLOCKS + 2 * k
            V[first:first + 2, :, 0:128] = rval[k].reshape(2, TILE, D)
            V[first:first + 2, :, 128:256] = cols[p * HALO:(p + 1) * HALO].reshape(2, TILE, 128)
            for h in range(2):
                at = p * HALO + h * TILE
                B[first + h] = far_b[:, at:at + TILE]
                lm[first + h] = far_lm[:, at:at + TILE]

    for k in range(4):
        o = OFFSETS[k]

        @pl.when((s + o >= 0) & (s + o < n_space))
        def _():
            for c in copies(k):
                c.wait_send()


def tile_kernel(codes, lmult, A, B, V, lm, acc_in, lat, w_in, wc2, rows, acc, upd_h, upd, wb, osem):
    total = lax.fori_loop(0, BLOCKS, lambda r, t: t + codes[r, 127], 0)

    def advance(state):
        out = []
        for _ in range(UNROLL):
            r, g = state
            over = g + 1 >= codes[r, 127]
            state = (jnp.minimum(jnp.where(over, r + 1, r), BLOCKS - 1), jnp.where(over, 0, g + 1))
            out.append(state)
        return out

    def weigh(q, r, g, it, sq):
        off = jnp.where(it * UNROLL + q < total, 0.0, NONE).astype(f32)
        for u in range(GROUP):
            level = lm[codes[r, g * GROUP + u]] + (lmult[r, g * GROUP + u] + off)
            d2 = jnp.maximum(sq[:, u * TILE:(u + 1) * TILE], 1e-12)
            wb[q, :, u * TILE:(u + 1) * TILE] = jnp.exp2(level - d2 * lax.rsqrt(d2)).astype(bf16)

    def distances(r, g):
        pair = jnp.concatenate([B[codes[r, g * GROUP + u]] for u in range(GROUP)], axis=1)
        return jnp.dot(A[r], pair, preferred_element_type=f32)

    def collect(q, r, g):
        sent = jnp.concatenate([V[codes[r, g * GROUP + u]] for u in range(GROUP)], axis=0)
        acc[r] = acc[r] + jnp.dot(wb[q], sent, preferred_element_type=f32)

    def step(it, last):
        now = tuple(advance(last[-1]))
        ahead = distances(*now[0])
        for q in range(UNROLL):
            collect(q, *last[q])
            sq = ahead
            if q + 1 < UNROLL:
                ahead = distances(*now[q + 1])
            weigh(q, *now[q], it, sq)
        return now

    zero = jnp.int32(0)
    first = tuple([(zero, zero)] + advance((zero, zero))[:UNROLL - 1])
    ahead = distances(*first[0])
    for q in range(UNROLL):
        sq = ahead
        if q + 1 < UNROLL:
            ahead = distances(*first[q + 1])
        weigh(q, *first[q], 0, sq)
    last = lax.fori_loop(1, (total + UNROLL - 1) // UNROLL, step, first)
    for q in range(UNROLL):
        collect(q, *last[q])

    bias_row = rows[0:1]
    gain_row = rows[1:2]
    PIECES = 8
    outs = [pltpu.make_async_copy(upd.at[pl.ds(i * (NODE // PIECES), NODE // PIECES)],
                                  upd_h.at[pl.ds(i * (NODE // PIECES), NODE // PIECES)], osem.at[i])
            for i in range(PIECES)]

    STEP = 2
    PARTS = BLOCKS // STEP

    def rows_of(p):
        return slice(p * STEP * TILE, (p + 1) * STEP * TILE)

    def stage1(p):
        got = acc[p * STEP:(p + 1) * STEP].reshape(STEP * TILE, 256)
        tot = got[:, 128:256]
        rs = lax.rsqrt(tot[:, 12:13])
        agg = (got[:, 0:128] * rs).astype(bf16)
        own = V[p * STEP:(p + 1) * STEP, :, 128:256].reshape(STEP * TILE, 128).astype(f32)
        q = tot * (rs * rs) - own
        qh = q.astype(bf16)
        qm = (q - qh.astype(f32)).astype(bf16)
        return jnp.concatenate([lat[rows_of(p)], agg, qh, qm], axis=1)

    def stage2(cat):
        pre = jnp.dot(cat, w_in[...], preferred_element_type=f32) + bias_row
        hid = (pre * (0.5 + 0.5 * jnp.tanh(0.5 * pre))).astype(bf16)
        return jnp.concatenate([hid, hid], axis=1)

    def stage3(p, hid):
        cen = jnp.dot(hid, wc2[...], preferred_element_type=f32)
        var = jnp.mean(cen * cen, axis=1, keepdims=True)
        out = lat[rows_of(p)].astype(f32) + cen * lax.rsqrt(var + 1e-5) * gain_row
        upd[rows_of(p)] = out.astype(bf16)

    cats, hids = {}, {}
    for p in range(PARTS + 2):
        if p >= 2:
            stage3(p - 2, hids.pop(p - 2))
            if (p - 1) % (PARTS // PIECES) == 0:
                outs[(p - 2) // (PARTS // PIECES)].start()
        if 1 <= p <= PARTS:
            hids[p - 1] = stage2(cats.pop(p - 1))
        if p < PARTS:
            cats[p] = stage1(p)
    for c in outs:
        c.wait()


NZ = 8
NY = 4


def pool_kernel(upd, want, out, hot, part, g1, a2, g2, a3, g3, full, s1, r1, s2, r2, s3, r3, s4, r4):
    s = lax.axis_index("space")
    f = lax.axis_index("frag")
    nf = lax.axis_size("frag")
    y = s // NZ
    z = lax.rem(s, NZ)
    barrier = pltpu.get_barrier_semaphore()

    def dev(dy, dz, df):
        return (lax.rem(y + dy, NY) * NZ + lax.rem(z + dz, NZ), lax.rem(f + df, nf))

    peers = [dev(0, 0, i) for i in range(1, nf)] + [dev(i, 0, 0) for i in range(1, NY)]
    peers += [dev(0, i, 0) for i in range(1, NZ)]
    for p in peers:
        pl.semaphore_signal(barrier, inc=1, device_id=p, device_id_type=MESH)

    def remote(src, dst, send, recv, i, to):
        return pltpu.make_async_remote_copy(
            src_ref=src, dst_ref=dst, send_sem=send.at[i - 1], recv_sem=recv.at[i - 1],
            device_id=to, device_id_type=MESH)

    c1 = {i: remote(part.at[i], g1.at[i - 1], s1, r1, i, dev(0, 0, i)) for i in range(1, nf)}
    c2 = {i: remote(a2.at[lax.rem(y + i, NY)], g2.at[i - 1], s2, r2, i, dev(i, 0, 0)) for i in range(1, NY)}
    c3 = {i: remote(a3, g3.at[i - 1], s3, r3, i, dev(0, i, 0)) for i in range(1, NZ)}
    c4 = {i: remote(full.at[y], full.at[y], s4, r4, i, dev(i, 0, 0)) for i in range(1, NY)}

    sub = lax.broadcasted_iota(i32, (FR_DEV, TILE), 0).astype(f32).astype(bf16)
    high = want[0:1]
    low = want[1:2]

    def build(slot, place, i):
        t = lax.rem(f + i, nf).astype(f32)
        row = jnp.where(high == t, low, -1.0).astype(bf16)
        for b in range(BLOCKS):
            cut = jnp.broadcast_to(row[:, b * TILE:(b + 1) * TILE], (FR_DEV, TILE))
            hot[slot, place * FR_DEV:(place + 1) * FR_DEV, b * TILE:(b + 1) * TILE] = jnp.where(
                cut == sub, 1.0, 0.0).astype(bf16)

    order = (4, 3, 5, 2, 6, 1, 7, 0)
    BATCH = 4
    for n in range(BATCH):
        build(0, n, order[n])
    for slot in range(nf // BATCH):
        if slot + 1 < nf // BATCH:
            for n in range(BATCH):
                build(slot + 1, n, order[(slot + 1) * BATCH + n])
        sums = jnp.dot(hot[slot], upd[...], preferred_element_type=f32)
        if slot == 0:
            pl.semaphore_wait(barrier, nf + NY + NZ - 3)
        for n in range(BATCH):
            i = order[slot * BATCH + n]
            mine = sums[n * FR_DEV:(n + 1) * FR_DEV]
            if i:
                part[i] = mine.astype(bf16)
                c1[i].start()
            else:
                total = mine
    for i in order[:-1]:
        c1[i].wait_recv()
        total = total + g1[i - 1].astype(f32)
    a2[...] = total.astype(bf16).reshape(NY, FR_DEV // NY, D)
    for i in (2, 1, 3):
        c2[i].start()
    total = a2[y].astype(f32)
    for i in (1, 3, 2):
        c2[i].wait_recv()
        total = total + g2[i - 1].astype(f32)
    a3[...] = total.astype(bf16)
    for i in (4, 3, 5, 2, 6, 1, 7):
        c3[i].start()
    total = a3[...].astype(f32)
    for i in (1, 7, 2, 6, 3, 5, 4):
        c3[i].wait_recv()
        total = total + g3[i - 1].astype(f32)
    full[y] = total
    for i in (2, 1, 3):
        c4[i].start()
    for i in (1, 3, 2):
        c4[i].wait_recv()
    out[...] = full[...].reshape(FR_DEV, D)
    for group in (c1, c2, c3, c4):
        for c in group.values():
            c.wait_send()


def shards(latents, positions, masses, w_value, w_self, w_message, w_offset, bias_hidden, w_out, norm_gain,
           tile_blocks, tile_count, send_rows, frag_ids):
    ns, nf = lax.axis_size("space"), lax.axis_size("frag")
    vm = pl.BlockSpec(memory_space=pltpu.VMEM)
    sm = pl.BlockSpec(memory_space=pltpu.SMEM)
    hbm = pl.BlockSpec(memory_space=pltpu.HBM)
    fa, fb = feature_maps()
    dma = pltpu.SemaphoreType.DMA
    vmem = pltpu.VMEM
    limit = 36 << 20
    pin = lambda a: pltpu.with_memory_space_constraint(a, pltpu.HBM)
    A, B, V, lm, codes, lmult, acc, lat, w_in, wc2, rows, want = pl.pallas_call(
        halo_kernel,
        out_shape=(
            jax.ShapeDtypeStruct((BLOCKS, TILE, 32), bf16),
            jax.ShapeDtypeStruct((EXT, 32, TILE), bf16),
            jax.ShapeDtypeStruct((EXT, TILE, 256), bf16),
            jax.ShapeDtypeStruct((EXT, 1, TILE), f32),
            jax.ShapeDtypeStruct((BLOCKS, 128), i32),
            jax.ShapeDtypeStruct((BLOCKS, 128), f32),
            jax.ShapeDtypeStruct((BLOCKS, TILE, 256), f32),
            jax.ShapeDtypeStruct((NODE, D), bf16),
            jax.ShapeDtypeStruct((512, D), bf16),
            jax.ShapeDtypeStruct((256, D), bf16),
            jax.ShapeDtypeStruct((2, D), f32),
            jax.ShapeDtypeStruct((2, NODE), f32),
        ),
        in_specs=[hbm] * 5 + [sm] + [hbm] * 10,
        out_specs=(vm,) * 12,
        scratch_shapes=[
            vmem((3, NODE), f32), vmem((1, NODE), f32), vmem((D, D), bf16),
            vmem((2, SLOTS), i32), vmem((4, HALO), i32), vmem((128, 32), bf16), vmem((32, 16), bf16),
            vmem((3, D), f32), vmem((D, D), bf16), vmem((1, NODE), i32),
            vmem((16, NODE), f32),
            vmem((HALO, NODE), bf16),
            vmem((4, HALO, D), bf16),
            vmem((4, 16, HALO), bf16),
            vmem((4, HALO, D), bf16),
            vmem((4, 16, HALO), bf16),
            dma((15,)),
            dma((2, 4)),
            dma((2, 4)),
        ],
        compiler_params=pltpu.CompilerParams(collective_id=0, has_side_effects=True, vmem_limit_bytes=limit),
    )(pin(latents), pin(positions), pin(masses.reshape(1, NODE)), pin(w_value), pin(tile_blocks), tile_count,
      pin(send_rows), pin(fa), pin(fb),
      pin(w_self), pin(w_message), pin(w_offset), pin(bias_hidden.reshape(1, D)), pin(w_out),
      pin(norm_gain.reshape(1, D)),
      pin(frag_ids.reshape(1, NODE)))

    _, updated, upd = pl.pallas_call(
        tile_kernel,
        out_shape=(
            jax.ShapeDtypeStruct((BLOCKS, TILE, 256), f32),
            jax.ShapeDtypeStruct((NODE, D), bf16),
            jax.ShapeDtypeStruct((NODE, D), bf16),
        ),
        in_specs=[sm, sm] + [vm] * 9,
        out_specs=(vm, hbm, vm),
        input_output_aliases={6: 0},
        scratch_shapes=[vmem((UNROLL, TILE, GROUP * TILE), bf16), dma((8,))],
        compiler_params=pltpu.CompilerParams(vmem_limit_bytes=limit),
    )(codes, lmult, A, B, V, lm, acc, lat, w_in, wc2, rows)

    pooled = pl.pallas_call(
        pool_kernel,
        out_shape=jax.ShapeDtypeStruct((FR_DEV, D), f32),
        in_specs=[vm, vm],
        out_specs=vm,
        scratch_shapes=[
            vmem((2, 4 * FR_DEV, NODE), bf16),
            vmem((nf, FR_DEV, D), bf16),
            vmem((nf - 1, FR_DEV, D), bf16),
            vmem((NY, FR_DEV // NY, D), bf16),
            vmem((NY - 1, FR_DEV // NY, D), bf16),
            vmem((FR_DEV // NY, D), bf16),
            vmem((NZ - 1, FR_DEV // NY, D), bf16),
            vmem((NY, FR_DEV // NY, D), f32),
            dma((nf - 1,)), dma((nf - 1,)),
            dma((NY - 1,)), dma((NY - 1,)),
            dma((NZ - 1,)), dma((NZ - 1,)),
            dma((NY - 1,)), dma((NY - 1,)),
        ],
        compiler_params=pltpu.CompilerParams(collective_id=1, has_side_effects=True, vmem_limit_bytes=limit),
    )(upd, want)
    return updated, pooled * math.sqrt(FR_DEV * nf / (NODE * ns * nf))


def solution(mesh):
    own = P(("space", "frag"))
    return jax.shard_map(
        shards,
        mesh=mesh,
        in_specs=(
            P(("space", "frag"), None), P(None, ("space", "frag")), own,
            P(), P(), P(), P(), P(), P(), P(),
            P(None, ("space", "frag")), own, P(None, ("space", "frag")), own,
        ),
        out_specs=(P(("space", "frag"), None), P("frag", None)),
        check_vma=False,
    )
```

```python
import math

import jax
import jax.numpy as jnp
import numpy as np
from jax import lax
from jax.experimental import pallas as pl
from jax.experimental.pallas import tpu as pltpu
from jax.sharding import PartitionSpec as P

D = 128
TILE = 128
REACH = 2
HALO = 256
BLOCKS = 32
EXT = 40
NODE = BLOCKS * TILE
SLOTS = 640
FR_DEV = 128
OFFSETS = tuple(o for o in range(-REACH, REACH + 1) if o != 0)
LOG2E = math.log2(math.e)
CENTRE = 6.0
GROUP = 2
UNROLL = 20
NONE = -1e30

f32, bf16, i32 = jnp.float32, jnp.bfloat16, jnp.int32
MESH = pl.DeviceIdType.MESH


def split3(x):
    high = x.astype(bf16).astype(f32)
    rest = x - high
    mid = rest.astype(bf16).astype(f32)
    return high, mid, rest - mid


def feature_maps():
    recv = np.zeros((128, 32), np.float32)
    send = np.zeros((32, 16), np.float32)
    pairs = ((0, 0), (0, 1), (1, 0), (1, 1), (0, 2), (2, 0))
    for p, (a, b) in enumerate(pairs):
        for c in range(3):
            recv[3 * a + c, 3 * p + c] = -2.0
            send[3 * p + c, 3 * b + c] = 1.0
    for c in range(3):
        recv[13 + c, 18 + c] = 1.0
        send[18 + c, 12] = 1.0
        recv[12, 21 + c] = 1.0
        send[21 + c, 13 + c] = 1.0
    return jnp.asarray(recv, bf16), jnp.asarray(send, bf16)


def aux_columns(rows):
    cols = jnp.transpose(jnp.concatenate([rows, rows], axis=0))
    return jnp.concatenate([cols, jnp.zeros((cols.shape[0], 96), f32)], axis=1)


def halo_kernel(lat_h, pos_h, mass_h, wv_h, tb_h, tc, sr_h, fa_h, fb_h,
                ws_h, wmsg_h, woff_h, bias_h, wo_h, gain_h, ids_h,
                A, B, V, lm, codes, lmult, acc, lat, w_in, wc2, rows_out, want,
                pos, mass, wv, tb, sr, fa, fb, w_offset, w_out, ids,
                rows_s, hot, sval, saux, rval, raux, isem, ssem, rsem):
    s = lax.axis_index("space")
    f = lax.axis_index("frag")
    n_space = lax.axis_size("space")
    loads = [pltpu.make_async_copy(src, dst, isem.at[i]) for i, (src, dst) in enumerate((
        (sr_h, sr), (pos_h, pos), (mass_h, mass), (lat_h, lat), (wv_h, wv), (tb_h, tb), (fa_h, fa), (fb_h, fb),
        (ws_h, w_in.at[0:128]), (wmsg_h, w_in.at[128:256]), (woff_h, w_offset), (wo_h, w_out),
        (bias_h, rows_out.at[0:1]), (gain_h, rows_out.at[1:2]), (ids_h, ids)))]
    for c in loads:
        c.start()
    barrier = pltpu.get_barrier_semaphore()
    for o in OFFSETS:
        @pl.when((s + o >= 0) & (s + o < n_space))
        def _():
            pl.semaphore_signal(barrier, inc=1, device_id=(s + o, f), device_id_type=MESH)

    loads[1].wait()
    loads[2].wait()
    x = (pos[...] - CENTRE) * LOG2E
    xh, xm, xl = split3(x)
    mh, mm, ml = split3(mass[...])
    sq = x * x
    norm = sq[0:1] + sq[1:2] + sq[2:3]
    nh, nm, nl = split3(norm)
    rows_s[...] = jnp.concatenate([xh, xm, xl, mh, mm, ml, jnp.ones((1, NODE), f32), nh, nm, nl], axis=0)
    for b in range(BLOCKS):
        V[b, :, 128:256] = aux_columns(rows_s[:, b * TILE:(b + 1) * TILE]).astype(bf16)
    loads[3].wait()
    loads[4].wait()
    loads[0].wait()
    values = jnp.dot(lat[...], wv[...], preferred_element_type=f32).astype(bf16)
    V[0:BLOCKS, :, 0:128] = values.reshape(BLOCKS, TILE, D)

    def copies(k):
        o = OFFSETS[k]
        dev = (s + o, f)
        return (
            pltpu.make_async_remote_copy(
                src_ref=sval.at[k], dst_ref=rval.at[k], send_sem=ssem.at[0, k], recv_sem=rsem.at[0, k],
                device_id=dev, device_id_type=MESH),
            pltpu.make_async_remote_copy(
                src_ref=saux.at[k], dst_ref=raux.at[k], send_sem=ssem.at[1, k], recv_sem=rsem.at[1, k],
                device_id=dev, device_id_type=MESH),
        )

    idx = sr[...].astype(f32)
    idx = jnp.transpose(jnp.concatenate([idx, idx], axis=0))
    lane = lax.broadcasted_iota(i32, (HALO, TILE), 1).astype(f32)
    for first, pair in ((True, (0,)), (False, (3,)), (False, (1,)), (False, (2,))):
        for p, k in enumerate(pair):
            col = idx[:, k:k + 1]
            high = jnp.floor(col * (1.0 / TILE))
            low = col - high * TILE
            code = jnp.where(low == lane, high, -1.0).astype(bf16)
            for b in range(BLOCKS):
                hot[p * HALO:(p + 1) * HALO, b * TILE:(b + 1) * TILE] = jnp.where(
                    code == jnp.asarray(b, bf16), 1.0, 0.0).astype(bf16)
        got = jnp.dot(hot[...], V[0:BLOCKS].reshape(NODE, 256), preferred_element_type=f32)
        if first:
            pl.semaphore_wait(barrier, jnp.minimum(s, REACH) + jnp.minimum(n_space - 1 - s, REACH))
        for p, k in enumerate(pair):
            part = got[p * HALO:(p + 1) * HALO]
            sval[k] = part[:, 0:128].astype(bf16)
            saux[k] = jnp.transpose(part[:, 128:256])[0:16].astype(bf16)
            o = OFFSETS[k]

            @pl.when((s + o >= 0) & (s + o < n_space))
            def _():
                for c in copies(k):
                    c.start()

            @pl.when((s - o < 0) | (s - o >= n_space))
            def _():
                rval[k] = jnp.zeros((HALO, D), bf16)
                raux[k] = jnp.zeros((16, HALO), bf16)

    for c in loads[5:]:
        c.wait()
    slot = lax.broadcasted_iota(i32, (BLOCKS, SLOTS), 1)
    rhot = (lax.broadcasted_iota(i32, (BLOCKS, SLOTS), 0) == tb[0:1, :]) & (slot < tc[0])
    chot = lax.broadcasted_iota(i32, (128, SLOTS), 0) == tb[1:2, :]
    count = lax.dot_general(
        jnp.where(rhot, 1.0, 0.0).astype(bf16), jnp.where(chot, 1.0, 0.0).astype(bf16),
        (((1,), (1,)), ((), ())), preferred_element_type=f32)
    live = jnp.where(count > 0.0, 1.0, 0.0)
    before = lax.broadcasted_iota(i32, (128, 128), 0) < lax.broadcasted_iota(i32, (128, 128), 1)
    place = jnp.dot(live.astype(bf16), jnp.where(before, 1.0, 0.0).astype(bf16), preferred_element_type=f32)
    place = jnp.where(count > 0.0, place, -1.0)
    col_id = lax.broadcasted_iota(i32, (BLOCKS, 128), 1).astype(f32)
    packed = col_id + 64.0 * count
    listed = jnp.zeros((BLOCKS, 128), f32)
    for c in range(EXT):
        listed = listed + jnp.where(place[:, c:c + 1] == col_id, packed[:, c:c + 1], 0.0)
    times = jnp.floor(listed * (1.0 / 64.0))
    sender = listed - 64.0 * times
    groups = jnp.maximum(jnp.floor((jnp.sum(live, axis=1, keepdims=True) + (GROUP - 1)) * (1.0 / GROUP)), 1.0)
    codes[...] = jnp.where(col_id == 127.0, groups, sender).astype(i32)
    lmult[...] = jnp.where(times > 0.0, jnp.log2(jnp.maximum(times, 1.0)), NONE)

    A[...] = jnp.dot(V[0:BLOCKS, :, 128:256].reshape(NODE, 128), fa[...],
                     preferred_element_type=f32).astype(bf16).reshape(BLOCKS, TILE, 32)
    own_b = jnp.dot(fb[...], rows_s[...].astype(bf16), preferred_element_type=f32).astype(bf16)
    lmass = jnp.log2(mass[...])
    for b in range(BLOCKS):
        B[b] = own_b[:, b * TILE:(b + 1) * TILE]
        lm[b] = lmass[:, b * TILE:(b + 1) * TILE]

    fid = ids[...].astype(f32)
    high = jnp.floor(fid * (1.0 / FR_DEV))
    want[0:1] = high
    want[1:2] = fid - high * FR_DEV
    woff = w_offset[...] * (1.0 / LOG2E)
    wh = woff.astype(bf16).astype(f32)
    wm = woff - wh
    w_in[256:384] = jnp.concatenate(
        [wh, wh, wh, jnp.zeros((7, 128), f32), wm, wm, wm, jnp.zeros((103, 128), f32)], axis=0).astype(bf16)
    w_in[384:512] = jnp.concatenate([wh, wh, wh, jnp.zeros((119, 128), f32)], axis=0).astype(bf16)
    wo = w_out[...].astype(f32)
    wc = wo - jnp.mean(wo, axis=1, keepdims=True)
    wc_h = wc.astype(bf16)
    wc2[0:128] = wc_h
    wc2[128:256] = (wc - wc_h.astype(f32)).astype(bf16)

    row_id = lax.broadcasted_iota(i32, (128, 128), 0)
    mass_map = jnp.where((row_id >= 9) & (row_id < 12), 1.0, 0.0).astype(bf16)
    for b in range(BLOCKS):
        own = V[b, :, 128:256]
        acc[b, :, 0:128] = jnp.zeros((TILE, 128), f32)
        acc[b, :, 128:256] = jnp.dot(own, mass_map, preferred_element_type=f32) * own.astype(f32)

    for pair in ((0, 3), (1, 2)):
        for k in pair:
            o = OFFSETS[k]

            @pl.when((s - o >= 0) & (s - o < n_space))
            def _():
                for c in copies(k):
                    c.wait_recv()

        aux = jnp.concatenate([raux[k] for k in pair], axis=1)
        far_b = jnp.dot(fb[...], aux, preferred_element_type=f32).astype(bf16)
        aux = aux.astype(f32)
        cols = aux_columns(aux).astype(bf16)
        far_mass = aux[9:10] + aux[10:11] + aux[11:12]
        far_lm = jnp.where(far_mass > 0.0, jnp.log2(jnp.maximum(far_mass, 1e-30)), NONE)
        for p, k in enumerate(pair):
            first = BLOCKS + 2 * k
            V[first:first + 2, :, 0:128] = rval[k].reshape(2, TILE, D)
            V[first:first + 2, :, 128:256] = cols[p * HALO:(p + 1) * HALO].reshape(2, TILE, 128)
            for h in range(2):
                at = p * HALO + h * TILE
                B[first + h] = far_b[:, at:at + TILE]
                lm[first + h] = far_lm[:, at:at + TILE]

    for k in range(4):
        o = OFFSETS[k]

        @pl.when((s + o >= 0) & (s + o < n_space))
        def _():
            for c in copies(k):
                c.wait_send()


def tile_kernel(codes, lmult, A, B, V, lm, acc_in, lat, w_in, wc2, rows, acc, upd_h, upd, wb, osem):
    total = lax.fori_loop(0, BLOCKS, lambda r, t: t + codes[r, 127], 0)

    def advance(state):
        out = []
        for _ in range(UNROLL):
            r, g = state
            over = g + 1 >= codes[r, 127]
            state = (jnp.minimum(jnp.where(over, r + 1, r), BLOCKS - 1), jnp.where(over, 0, g + 1))
            out.append(state)
        return out

    def weigh(q, r, g, it, sq):
        off = jnp.where(it * UNROLL + q < total, 0.0, NONE).astype(f32)
        for u in range(GROUP):
            level = lm[codes[r, g * GROUP + u]] + (lmult[r, g * GROUP + u] + off)
            d2 = jnp.maximum(sq[:, u * TILE:(u + 1) * TILE], 1e-12)
            wb[q, :, u * TILE:(u + 1) * TILE] = jnp.exp2(level - d2 * lax.rsqrt(d2)).astype(bf16)

    def distances(r, g):
        pair = jnp.concatenate([B[codes[r, g * GROUP + u]] for u in range(GROUP)], axis=1)
        return jnp.dot(A[r], pair, preferred_element_type=f32)

    def collect(q, r, g):
        sent = jnp.concatenate([V[codes[r, g * GROUP + u]] for u in range(GROUP)], axis=0)
        acc[r] = acc[r] + jnp.dot(wb[q], sent, preferred_element_type=f32)

    def step(it, last):
        now = tuple(advance(last[-1]))
        ahead = distances(*now[0])
        for q in range(UNROLL):
            collect(q, *last[q])
            sq = ahead
            if q + 1 < UNROLL:
                ahead = distances(*now[q + 1])
            weigh(q, *now[q], it, sq)
        return now

    zero = jnp.int32(0)
    first = tuple([(zero, zero)] + advance((zero, zero))[:UNROLL - 1])
    ahead = distances(*first[0])
    for q in range(UNROLL):
        sq = ahead
        if q + 1 < UNROLL:
            ahead = distances(*first[q + 1])
        weigh(q, *first[q], 0, sq)
    last = lax.fori_loop(1, (total + UNROLL - 1) // UNROLL, step, first)
    for q in range(UNROLL):
        collect(q, *last[q])

    bias_row = rows[0:1]
    gain_row = rows[1:2]
    PIECES = 8
    outs = [pltpu.make_async_copy(upd.at[pl.ds(i * (NODE // PIECES), NODE // PIECES)],
                                  upd_h.at[pl.ds(i * (NODE // PIECES), NODE // PIECES)], osem.at[i])
            for i in range(PIECES)]

    STEP = 2
    PARTS = BLOCKS // STEP

    def rows_of(p):
        return slice(p * STEP * TILE, (p + 1) * STEP * TILE)

    def stage1(p):
        got = acc[p * STEP:(p + 1) * STEP].reshape(STEP * TILE, 256)
        tot = got[:, 128:256]
        rs = lax.rsqrt(tot[:, 12:13])
        agg = (got[:, 0:128] * rs).astype(bf16)
        own = V[p * STEP:(p + 1) * STEP, :, 128:256].reshape(STEP * TILE, 128).astype(f32)
        q = tot * (rs * rs) - own
        qh = q.astype(bf16)
        qm = (q - qh.astype(f32)).astype(bf16)
        return jnp.concatenate([lat[rows_of(p)], agg, qh, qm], axis=1)

    def stage2(cat):
        pre = jnp.dot(cat, w_in[...], preferred_element_type=f32) + bias_row
        hid = (pre * (0.5 + 0.5 * jnp.tanh(0.5 * pre))).astype(bf16)
        return jnp.concatenate([hid, hid], axis=1)

    def stage3(p, hid):
        cen = jnp.dot(hid, wc2[...], preferred_element_type=f32)
        var = jnp.mean(cen * cen, axis=1, keepdims=True)
        out = lat[rows_of(p)].astype(f32) + cen * lax.rsqrt(var + 1e-5) * gain_row
        upd[rows_of(p)] = out.astype(bf16)

    cats, hids = {}, {}
    for p in range(PARTS + 2):
        if p >= 2:
            stage3(p - 2, hids.pop(p - 2))
            if (p - 1) % (PARTS // PIECES) == 0:
                outs[(p - 2) // (PARTS // PIECES)].start()
        if 1 <= p <= PARTS:
            hids[p - 1] = stage2(cats.pop(p - 1))
        if p < PARTS:
            cats[p] = stage1(p)
    for c in outs:
        c.wait()


NZ = 8
NY = 4


def pool_kernel(upd, want, out, hot, part, g1, a2, g2, a3, g3, full, s1, r1, s2, r2, s3, r3, s4, r4):
    s = lax.axis_index("space")
    f = lax.axis_index("frag")
    nf = lax.axis_size("frag")
    y = s // NZ
    z = lax.rem(s, NZ)
    barrier = pltpu.get_barrier_semaphore()

    def dev(dy, dz, df):
        return (lax.rem(y + dy, NY) * NZ + lax.rem(z + dz, NZ), lax.rem(f + df, nf))

    peers = [dev(0, 0, i) for i in range(1, nf)] + [dev(i, 0, 0) for i in range(1, NY)]
    peers += [dev(0, i, 0) for i in range(1, NZ)]
    for p in peers:
        pl.semaphore_signal(barrier, inc=1, device_id=p, device_id_type=MESH)

    def remote(src, dst, send, recv, i, to):
        return pltpu.make_async_remote_copy(
            src_ref=src, dst_ref=dst, send_sem=send.at[i - 1], recv_sem=recv.at[i - 1],
            device_id=to, device_id_type=MESH)

    c1 = {i: remote(part.at[i], g1.at[i - 1], s1, r1, i, dev(0, 0, i)) for i in range(1, nf)}
    c2 = {i: remote(a2.at[lax.rem(y + i, NY)], g2.at[i - 1], s2, r2, i, dev(i, 0, 0)) for i in range(1, NY)}
    c3 = {i: remote(a3, g3.at[i - 1], s3, r3, i, dev(0, i, 0)) for i in range(1, NZ)}
    c4 = {i: remote(full.at[y], full.at[y], s4, r4, i, dev(i, 0, 0)) for i in range(1, NY)}

    sub = lax.broadcasted_iota(i32, (FR_DEV, TILE), 0).astype(f32).astype(bf16)
    high = want[0:1]
    low = want[1:2]

    def build(slot, place, i):
        t = lax.rem(f + i, nf).astype(f32)
        row = jnp.where(high == t, low, -1.0).astype(bf16)
        for b in range(BLOCKS):
            cut = jnp.broadcast_to(row[:, b * TILE:(b + 1) * TILE], (FR_DEV, TILE))
            hot[slot, place * FR_DEV:(place + 1) * FR_DEV, b * TILE:(b + 1) * TILE] = jnp.where(
                cut == sub, 1.0, 0.0).astype(bf16)

    order = (4, 3, 5, 2, 6, 1, 7, 0)
    BATCH = 4
    for n in range(BATCH):
        build(0, n, order[n])
    for slot in range(nf // BATCH):
        if slot + 1 < nf // BATCH:
            for n in range(BATCH):
                build(slot + 1, n, order[(slot + 1) * BATCH + n])
        sums = jnp.dot(hot[slot], upd[...], preferred_element_type=f32)
        if slot == 0:
            pl.semaphore_wait(barrier, nf + NY + NZ - 3)
        for n in range(BATCH):
            i = order[slot * BATCH + n]
            mine = sums[n * FR_DEV:(n + 1) * FR_DEV]
            if i:
                part[i] = mine.astype(bf16)
                c1[i].start()
            else:
                total = mine
    for i in order[:-1]:
        c1[i].wait_recv()
        total = total + g1[i - 1].astype(f32)
    a2[...] = total.astype(bf16).reshape(NY, FR_DEV // NY, D)
    for i in (2, 1, 3):
        c2[i].start()
    total = a2[y].astype(f32)
    for i in (1, 3, 2):
        c2[i].wait_recv()
        total = total + g2[i - 1].astype(f32)
    a3[...] = total.astype(bf16)
    for i in (4, 3, 5, 2, 6, 1, 7):
        c3[i].start()
    total = a3[...].astype(f32)
    for i in (1, 7, 2, 6, 3, 5, 4):
        c3[i].wait_recv()
        total = total + g3[i - 1].astype(f32)
    full[y] = total
    for i in (2, 1, 3):
        c4[i].start()
    for i in (1, 3, 2):
        c4[i].wait_recv()
    out[...] = full[...].reshape(FR_DEV, D)
    for group in (c1, c2, c3, c4):
        for c in group.values():
            c.wait_send()


def shards(latents, positions, masses, w_value, w_self, w_message, w_offset, bias_hidden, w_out, norm_gain,
           tile_blocks, tile_count, send_rows, frag_ids):
    ns, nf = lax.axis_size("space"), lax.axis_size("frag")
    vm = pl.BlockSpec(memory_space=pltpu.VMEM)
    sm = pl.BlockSpec(memory_space=pltpu.SMEM)
    hbm = pl.BlockSpec(memory_space=pltpu.HBM)
    fa, fb = feature_maps()
    dma = pltpu.SemaphoreType.DMA
    vmem = pltpu.VMEM
    limit = 36 << 20
    pin = lambda a: pltpu.with_memory_space_constraint(a, pltpu.HBM)
    A, B, V, lm, codes, lmult, acc, lat, w_in, wc2, rows, want = pl.pallas_call(
        halo_kernel,
        out_shape=(
            jax.ShapeDtypeStruct((BLOCKS, TILE, 32), bf16),
            jax.ShapeDtypeStruct((EXT, 32, TILE), bf16),
            jax.ShapeDtypeStruct((EXT, TILE, 256), bf16),
            jax.ShapeDtypeStruct((EXT, 1, TILE), f32),
            jax.ShapeDtypeStruct((BLOCKS, 128), i32),
            jax.ShapeDtypeStruct((BLOCKS, 128), f32),
            jax.ShapeDtypeStruct((BLOCKS, TILE, 256), f32),
            jax.ShapeDtypeStruct((NODE, D), bf16),
            jax.ShapeDtypeStruct((512, D), bf16),
            jax.ShapeDtypeStruct((256, D), bf16),
            jax.ShapeDtypeStruct((2, D), f32),
            jax.ShapeDtypeStruct((2, NODE), f32),
        ),
        in_specs=[hbm] * 5 + [sm] + [hbm] * 10,
        out_specs=(vm,) * 12,
        scratch_shapes=[
            vmem((3, NODE), f32), vmem((1, NODE), f32), vmem((D, D), bf16),
            vmem((2, SLOTS), i32), vmem((4, HALO), i32), vmem((128, 32), bf16), vmem((32, 16), bf16),
            vmem((3, D), f32), vmem((D, D), bf16), vmem((1, NODE), i32),
            vmem((16, NODE), f32),
            vmem((HALO, NODE), bf16),
            vmem((4, HALO, D), bf16),
            vmem((4, 16, HALO), bf16),
            vmem((4, HALO, D), bf16),
            vmem((4, 16, HALO), bf16),
            dma((15,)),
            dma((2, 4)),
            dma((2, 4)),
        ],
        compiler_params=pltpu.CompilerParams(collective_id=0, has_side_effects=True, vmem_limit_bytes=limit),
    )(pin(latents), pin(positions), pin(masses.reshape(1, NODE)), pin(w_value), pin(tile_blocks), tile_count,
      pin(send_rows), pin(fa), pin(fb),
      pin(w_self), pin(w_message), pin(w_offset), pin(bias_hidden.reshape(1, D)), pin(w_out),
      pin(norm_gain.reshape(1, D)),
      pin(frag_ids.reshape(1, NODE)))

    _, updated, upd = pl.pallas_call(
        tile_kernel,
        out_shape=(
            jax.ShapeDtypeStruct((BLOCKS, TILE, 256), f32),
            jax.ShapeDtypeStruct((NODE, D), bf16),
            jax.ShapeDtypeStruct((NODE, D), bf16),
        ),
        in_specs=[sm, sm] + [vm] * 9,
        out_specs=(vm, hbm, vm),
        input_output_aliases={6: 0},
        scratch_shapes=[vmem((UNROLL, TILE, GROUP * TILE), bf16), dma((8,))],
        compiler_params=pltpu.CompilerParams(vmem_limit_bytes=limit),
    )(codes, lmult, A, B, V, lm, acc, lat, w_in, wc2, rows)

    pooled = pl.pallas_call(
        pool_kernel,
        out_shape=jax.ShapeDtypeStruct((FR_DEV, D), f32),
        in_specs=[vm, vm],
        out_specs=vm,
        scratch_shapes=[
            vmem((2, 4 * FR_DEV, NODE), bf16),
            vmem((nf, FR_DEV, D), bf16),
            vmem((nf - 1, FR_DEV, D), bf16),
            vmem((NY, FR_DEV // NY, D), bf16),
            vmem((NY - 1, FR_DEV // NY, D), bf16),
            vmem((FR_DEV // NY, D), bf16),
            vmem((NZ - 1, FR_DEV // NY, D), bf16),
            vmem((NY, FR_DEV // NY, D), f32),
            dma((nf - 1,)), dma((nf - 1,)),
            dma((NY - 1,)), dma((NY - 1,)),
            dma((NZ - 1,)), dma((NZ - 1,)),
            dma((NY - 1,)), dma((NY - 1,)),
        ],
        compiler_params=pltpu.CompilerParams(collective_id=1, has_side_effects=True, vmem_limit_bytes=limit),
    )(upd, want)
    return updated, pooled * math.sqrt(FR_DEV * nf / (NODE * ns * nf))


def solution(mesh):
    own = P(("space", "frag"))
    return jax.shard_map(
        shards,
        mesh=mesh,
        in_specs=(
            P(("space", "frag"), None), P(None, ("space", "frag")), own,
            P(), P(), P(), P(), P(), P(), P(),
            P(None, ("space", "frag")), own, P(None, ("space", "frag")), own,
        ),
        out_specs=(P(("space", "frag"), None), P("frag", None)),
        check_vma=False,
    )
```
